1024 devices in a mesh: sec: 2 (over core), tile: 512 (over x, z, y).
Axes of the slice: x: 4, y: 4, z: 32, core: 2. Of those that a mesh axis runs over, the one named last changes fastest.
Arguments:
- object_field: bfloat16 [2, 2, 131072, 512], P(None, 'sec', 'tile'), may hold values from -1 to 1
- probe: bfloat16 [2, 256, 256], replicated, may hold values from -6 to 6
- phases: float32 [256], replicated, may hold values from -3.140625 to 3.140625
- intensities: bfloat16 [1024, 256, 256], P('tile'), may hold values from 0.099609375 to 2
- pos_row: int32 [1024], P('tile'), may hold values from 0 to 255
- pos_col: int32 [1024], P('tile'), may hold values from 0 to 256
- counts: int32 [512], P('tile'), may hold values from 1 to 2, as said below
Outputs:
- object_gradient: float32 [2, 2, 131072, 512], P(None, 'sec', 'tile')
The draws below stay inside these ranges and needn't reach their ends.
Inputs may be any that keep to these rules, and one draw needn't show every extreme that they name: `counts`: every strip has at least one live position, and some strip has exactly 2 in every draw.
All inputs are finite; a program needn't handle non-finite values.
Results may differ from the reference program's by a relative error of at most 0.025.
Values may be sent and summed in bfloat16 or wider, within the bound.
A program may use at most 64 MiB of HBM per device.

```python
import math
import jax
import jax.numpy as jnp
from jax import lax

WAVE = 256
P_DEV = 2
COLS = 512
SLICES = 2
TILES = 512
NX = 131072
POS = 1024


def draw_counts(key, part):
    base_count = jax.random.randint(jax.random.fold_in(key, 1), (TILES,), 1, max(P_DEV // 2, 1) + 1)
    full_tile = jax.random.randint(jax.random.fold_in(key, 2), (TILES,), 0, 8) == 0
    chosen = jax.random.randint(jax.random.fold_in(key, 3), (), 0, TILES)
    position_ids = jnp.arange(TILES, dtype=jnp.int32)
    return jnp.where(full_tile | (position_ids == chosen), P_DEV, base_count).astype(jnp.int32)


def plant(values, own_key, least, high):
    dims = values.shape
    index_at = [jax.random.randint(jax.random.fold_in(own_key, axis), (), 0, dims[axis]) for axis in range(len(dims))]
    values = values.at[tuple(index_at)].set(least)
    longest = dims.index(max(dims))
    index_at[longest] = (index_at[longest] + 1) % dims[longest]
    return values.at[tuple(index_at)].set(high)


def level_of(key, dims, shards, least, high):
    loudness, own = 1.0, jax.random.fold_in(key, 6)
    for axis_at, blocks in shards:
        steps = jnp.exp(jax.random.uniform(jax.random.fold_in(own, axis_at), (blocks,), jnp.float32, least / len(shards), high / len(shards)))
        loudness = loudness * jnp.repeat(steps, dims[axis_at] // blocks).reshape([-1 if axis == axis_at else 1 for axis in range(len(dims))])
    return loudness


def normal_values(stream_key, dims, scale, bound, kind=jnp.bfloat16):
    array = scale * jax.random.normal(stream_key, dims, jnp.float32)
    return jnp.clip(array, min=-bound, max=bound).astype(kind)


def setup_inputs(seed: int = 0) -> dict:
    streams_of = jax.random.split(jax.random.key(seed), 8)
    object_field = jnp.clip(jax.random.uniform(streams_of[0], (2, SLICES, NX, COLS), jnp.float32, -1.0, 1.0) * level_of(streams_of[0], (2, SLICES, NX, COLS), ((1, 2), (2, 512)), -0.4, 0.0), -1.0, 1.0).astype(jnp.bfloat16)
    probe = normal_values(streams_of[1], (2, WAVE, WAVE), 1.0, 6.0)
    phases = jnp.clip(jax.random.uniform(streams_of[2], (WAVE,), jnp.float32, -3.140625, 3.140625), -3.140625, 3.140625)
    intensities = jnp.clip(jnp.exp(math.log(2.0) - 2.9996462 * jax.random.uniform(streams_of[3], (POS, WAVE, WAVE), jnp.float32) ** level_of(streams_of[3], (POS, WAVE, WAVE), ((0, 512),), -0.2, 0.2)), 0.099609375, 2.0).astype(jnp.bfloat16)
    pos_row = plant(jax.random.randint(streams_of[4], (POS,), 0, WAVE), jax.random.fold_in(streams_of[4], 1), 0, WAVE - 1).astype(jnp.int32)
    pos_col = plant(jax.random.randint(streams_of[5], (POS,), 0, COLS - WAVE + 1), jax.random.fold_in(streams_of[5], 1), 0, COLS - WAVE).astype(jnp.int32)
    counts = draw_counts(jax.random.fold_in(streams_of[7], 71), 0)
    return dict(object_field=object_field, probe=probe, phases=phases, intensities=intensities, pos_row=pos_row, pos_col=pos_col, counts=counts)


def build_tables(phases, wave_side):
    frequency = jnp.arange(wave_side, dtype=jnp.int32)
    product = frequency[:, None] * frequency[None, :] % wave_side
    angles = product.astype(jnp.float32) * (2.0 * math.pi / wave_side)
    cosine = jnp.cos(angles)
    sine_table = jnp.sin(angles)
    turned = phases[:, None] + angles
    turned_re = jnp.cos(turned)
    turned_im = jnp.sin(turned)
    highest = lax.Precision.HIGHEST
    kernel_re = (jnp.dot(turned_re.T, cosine, precision=highest, preferred_element_type=jnp.float32) + jnp.dot(turned_im.T, sine_table, precision=highest, preferred_element_type=jnp.float32)) / wave_side
    kernel_im = (jnp.dot(turned_im.T, cosine, precision=highest, preferred_element_type=jnp.float32) - jnp.dot(turned_re.T, sine_table, precision=highest, preferred_element_type=jnp.float32)) / wave_side
    norm_scale = 1.0 / math.sqrt(wave_side)
    far_re = cosine * norm_scale
    far_im = -sine_table * norm_scale
    return (kernel_re.astype(jnp.bfloat16), kernel_im.astype(jnp.bfloat16), far_re.astype(jnp.bfloat16), far_im.astype(jnp.bfloat16))

def left_product(matrix, field):
    return jnp.einsum('mj,bjn->bmn', matrix.astype(jnp.float32), field.astype(jnp.float32), precision=lax.Precision.HIGHEST)

def right_product(field, matrix):
    return jnp.einsum('bmj,nj->bmn', field.astype(jnp.float32), matrix.astype(jnp.float32), precision=lax.Precision.HIGHEST)

def propagate(matrix_re, matrix_im, field_re, field_im):
    inner_re = (left_product(matrix_re, field_re) - left_product(matrix_im, field_im)).astype(jnp.bfloat16)
    inner_im = (left_product(matrix_re, field_im) + left_product(matrix_im, field_re)).astype(jnp.bfloat16)
    outer_re = (right_product(inner_re, matrix_re) - right_product(inner_im, matrix_im)).astype(jnp.bfloat16)
    outer_im = (right_product(inner_re, matrix_im) + right_product(inner_im, matrix_re)).astype(jnp.bfloat16)
    return (outer_re, outer_im)

def transmit(trans_re, trans_im, wave_re, wave_im):
    t_re = trans_re.astype(jnp.float32)
    t_im = trans_im.astype(jnp.float32)
    w_re = wave_re.astype(jnp.float32)
    w_im = wave_im.astype(jnp.float32)
    return ((t_re * w_re - t_im * w_im).astype(jnp.bfloat16), (t_re * w_im + t_im * w_re).astype(jnp.bfloat16))

def conj_times(first_re, first_im, second_re, second_im):
    a_re = first_re.astype(jnp.float32)
    a_im = first_im.astype(jnp.float32)
    b_re = second_re.astype(jnp.float32)
    b_im = second_im.astype(jnp.float32)
    return (a_re * b_re + a_im * b_im, a_re * b_im - a_im * b_re)

def reference(object_field, probe, phases, intensities, pos_row, pos_col, counts):
    kernel_re, kernel_im, far_re, far_im = build_tables(phases, WAVE)
    matrices = []
    for layer_index in range(SLICES):
        if layer_index == SLICES - 1:
            matrices.append((far_re, far_im))
        else:
            matrices.append((kernel_re, kernel_im))
    padded = jnp.concatenate([object_field, jnp.zeros((2, SLICES, WAVE, COLS), jnp.bfloat16)], axis=2)
    gradient = jnp.zeros((2, SLICES, NX + WAVE, COLS), jnp.float32)
    anchor = jnp.zeros((), jnp.int32)

    def per_tile(gradient, tile_index):
        first_slot = (tile_index * P_DEV).astype(jnp.int32)
        row_offsets = lax.dynamic_slice_in_dim(pos_row, first_slot, P_DEV)
        col_offsets = lax.dynamic_slice_in_dim(pos_col, first_slot, P_DEV)
        measured = lax.dynamic_slice_in_dim(intensities, first_slot, P_DEV, 0).astype(jnp.float32)
        weights = (jnp.arange(P_DEV, dtype=jnp.int32) < counts[tile_index]).astype(jnp.float32)
        starts = (tile_index * WAVE + row_offsets).astype(jnp.int32)

        def cut_window(top_row, left_col):
            return lax.dynamic_slice(padded, (anchor, anchor, top_row, left_col), (2, SLICES, WAVE, WAVE))
        windows = jax.vmap(cut_window)(starts, col_offsets)
        wave_re = jnp.broadcast_to(probe[0], (P_DEV, WAVE, WAVE))
        wave_im = jnp.broadcast_to(probe[1], (P_DEV, WAVE, WAVE))
        entries = []
        for layer_index in range(SLICES):
            entries.append((wave_re, wave_im))
            mixed_re, mixed_im = transmit(windows[:, 0, layer_index], windows[:, 1, layer_index], wave_re, wave_im)
            wave_re, wave_im = propagate(matrices[layer_index][0], matrices[layer_index][1], mixed_re, mixed_im)
        leave_re = wave_re.astype(jnp.float32)
        leave_im = wave_im.astype(jnp.float32)
        factor = 2.0 * (leave_re * leave_re + leave_im * leave_im - measured) * weights[:, None, None]
        back_re = (factor * leave_re).astype(jnp.bfloat16)
        back_im = (factor * leave_im).astype(jnp.bfloat16)
        patch_re = [None] * SLICES
        patch_im = [None] * SLICES
        for layer_index in reversed(range(SLICES)):
            matrix_re, matrix_im = matrices[layer_index]
            spread_re, spread_im = propagate(matrix_re.T, -matrix_im.T, back_re, back_im)
            enter_re, enter_im = entries[layer_index]
            patch_re[layer_index], patch_im[layer_index] = conj_times(enter_re, enter_im, spread_re, spread_im)
            if layer_index > 0:
                next_re, next_im = conj_times(windows[:, 0, layer_index], windows[:, 1, layer_index], spread_re, spread_im)
                back_re = next_re.astype(jnp.bfloat16)
                back_im = next_im.astype(jnp.bfloat16)
        patches = jnp.stack([jnp.stack(patch_re, axis=1), jnp.stack(patch_im, axis=1)], axis=1)
        for member in range(P_DEV):
            corner = (anchor, anchor, starts[member], col_offsets[member])
            current = lax.dynamic_slice(gradient, corner, (2, SLICES, WAVE, WAVE))
            gradient = lax.dynamic_update_slice(gradient, current + patches[member], corner)
        return (gradient, None)
    gradient, ignored = lax.scan(per_tile, gradient, jnp.arange(TILES, dtype=jnp.int32))
    return gradient[:, :, :NX]
```

```python
import functools
import math

import jax
import jax.numpy as jnp
import numpy as np
from jax import lax
from jax.experimental import pallas as pl
from jax.experimental.pallas import tpu as pltpu
from jax.sharding import PartitionSpec as P

MESH = pl.DeviceIdType.MESH
F32 = jnp.float32
BF16 = jnp.bfloat16


def dot(a, b):
    return jnp.dot(a, b, preferred_element_type=F32)


def exact_dot(a, b):
    return jnp.dot(a, b, precision=lax.Precision.HIGHEST, preferred_element_type=F32)


def angle_tables(side):
    index = np.arange(side, dtype=np.int64)
    angles = (index[:, None] * index[None, :] % side) * (2.0 * math.pi / side)
    return np.cos(angles).astype(np.float32), np.sin(angles).astype(np.float32)


def kernel(
    tiles,
    side,
    row_ref,
    col_ref,
    count_ref,
    object_hbm,
    probe_hbm,
    turn_hbm,
    measured_hbm,
    cosine_hbm,
    sine_hbm,
    out_ref,
    field,
    probe,
    turn,
    cosine,
    sine,
    measured,
    mine,
    prev,
    send_core,
    send_prev,
    send_next,
    own,
    far,
    kl,
    klt,
    flr,
    flrt,
    flc,
    flct,
    psi0,
    psi1,
    grad,
    grad_core,
    grad_far,
    load_sem,
    scalar_sem,
    core_sem,
    prev_sem,
    next_sem,
    far_sem,
    measured_send,
    measured_sem,
    grad_core_sem,
    grad_send,
    grad_far_sem,
):
    sec = lax.axis_index("sec")
    tile = lax.axis_index("tile")
    other = 1 - sec
    before = lax.rem(tile + tiles - 1, tiles)
    after = lax.rem(tile + 1, tiles)
    half = side // 2

    loads = [
        pltpu.make_async_copy(object_hbm.at[:, 0], field, load_sem.at[0]),
        pltpu.make_async_copy(probe_hbm, probe, load_sem.at[1]),
        pltpu.make_async_copy(turn_hbm, turn, load_sem.at[2]),
        pltpu.make_async_copy(cosine_hbm, cosine, load_sem.at[3]),
        pltpu.make_async_copy(sine_hbm, sine, load_sem.at[4]),
    ]
    for load in loads:
        load.start()

    barrier = pltpu.get_barrier_semaphore()
    partners = [(other, tile), (0, before), (1, before), (0, after), (1, after)]
    for partner in partners:
        pl.semaphore_signal(barrier, inc=1, device_id=partner, device_id_type=MESH)

    line = lax.broadcasted_iota(jnp.int32, (8, side), 0)
    values = jnp.zeros((8, side), jnp.int32)
    for at, value in enumerate((row_ref[0], row_ref[1], col_ref[0], col_ref[1], count_ref[0])):
        values = jnp.where(line == at, value, values)
    mine[...] = values
    pl.semaphore_wait(barrier, len(partners))

    scalars = pltpu.make_async_remote_copy(
        mine, prev, scalar_sem.at[0], scalar_sem.at[1], device_id=(sec, after), device_id_type=MESH
    )
    scalars.start()

    def remote(source, target, send, receive, device):
        return pltpu.make_async_remote_copy(
            source, target, send, receive, device_id=device, device_id_type=MESH
        )

    first = sec == 0
    column = lax.broadcasted_iota(jnp.int32, (side, side), 1)
    row = lax.broadcasted_iota(jnp.int32, (side, side), 0)

    def pick(target, left_col):
        turned = column < left_col
        for part in range(2):
            target[part] = jnp.where(turned, field[part, :, side:], field[part, :, :side])

    loads[0].wait()
    own_vec = (mine[0:1, :], mine[1:2, :], mine[2:3, :], mine[3:4, :], mine[4:5, :])
    pick(send_next, own_vec[3])
    to_next = remote(send_next, far.at[sec], next_sem.at[0], far_sem.at[sec], (1, after))
    to_next.start()
    scalars.wait()
    prev_vec = (prev[0:1, :], prev[1:2, :], prev[2:3, :], prev[3:4, :], prev[4:5, :])
    pick(send_prev, prev_vec[2])
    to_prev = remote(send_prev, far.at[sec], prev_sem.at[0], far_sem.at[sec], (0, before))
    to_prev.start()
    rows_part = pl.ds(pl.multiple_of(sec * half, half), half)
    intensity = remote(
        measured_hbm.at[1, rows_part],
        measured.at[rows_part],
        measured_send.at[0],
        measured_sem.at[sec],
        (1, after),
    )
    intensity.start()
    local_intensity = pltpu.make_async_copy(measured_hbm.at[0], measured, load_sem.at[5])

    @pl.when(first)
    def _():
        local_intensity.start()

    my_row = jnp.where(first, own_vec[0], prev_vec[1])
    my_col = jnp.where(first, own_vec[2], prev_vec[3])
    live = jnp.where(first, (own_vec[4] > 0).astype(F32), (prev_vec[4] > 1).astype(F32))
    their_col = jnp.where(first, prev_vec[3], own_vec[2])
    their_row = jnp.where(first, prev_vec[1], own_vec[0])

    pick(send_core, their_col)
    to_core = remote(send_core, own.at[sec], core_sem.at[0], core_sem.at[1], (other, tile))
    to_core.start()
    pick(own.at[sec], my_col)

    for load in loads[1:]:
        load.wait()
    cos_table = cosine[...]
    sin_table = sine[...]
    phase = turn[...]
    phase_cos = jnp.cos(phase)
    phase_sin = jnp.sin(phase)
    turned_re = cos_table * phase_cos - sin_table * phase_sin
    turned_im = sin_table * phase_cos + cos_table * phase_sin
    scale = 1.0 / side
    k_re = (exact_dot(turned_re, cos_table) + exact_dot(turned_im, sin_table)) * scale
    k_im = (exact_dot(turned_im, cos_table) - exact_dot(turned_re, sin_table)) * scale

    def fill(target, re, im):
        target[:side, :side] = re
        target[:side, side:] = -im
        target[side:, :side] = im
        target[side:, side:] = re

    fill(kl, k_re.astype(BF16), k_im.astype(BF16))
    fill(klt, k_re.T.astype(BF16), -(k_im.T).astype(BF16))

    def one_hot(difference, shift):
        return ((difference & (side - 1)) == (shift & (side - 1))).astype(F32).astype(BF16)

    roll_rows = one_hot(row - column, my_row)
    roll_rows_t = one_hot(column - row, my_row)
    roll_cols = one_hot(row - column, my_col)
    roll_cols_t = one_hot(column - row, my_col)
    norm_scale = 1.0 / math.sqrt(side)
    far_re = (cos_table * norm_scale).astype(BF16)
    far_im = (-sin_table * norm_scale).astype(BF16)
    fill(flr, dot(far_re, roll_rows_t).astype(BF16), dot(far_im, roll_rows_t).astype(BF16))
    fill(flrt, dot(roll_rows, far_re).astype(BF16), -dot(roll_rows, far_im).astype(BF16))
    fill(flc, dot(far_re, roll_cols_t).astype(BF16), dot(far_im, roll_cols_t).astype(BF16))
    fill(flct, dot(roll_cols, far_re).astype(BF16), -dot(roll_cols, far_im).astype(BF16))
    for part in range(2):
        half_way = dot(roll_rows, probe[part]).astype(BF16)
        psi0[part] = dot(half_way, roll_cols_t).astype(BF16)

    in_next = row < my_row
    mine_rows = in_next != first
    in_mine = jnp.where(mine_rows, 1.0, 0.0)
    edge_first = first & (tile == tiles - 1)
    edge_second = jnp.logical_not(first) & (tile == 0)
    own_gate = in_mine * jnp.where(edge_second, 0.0, 1.0)
    far_gate = (1.0 - in_mine) * jnp.where(edge_first, 0.0, 1.0)

    def window(layer):
        return [
            own[layer, part].astype(F32) * own_gate + far[layer, part].astype(F32) * far_gate
            for part in range(2)
        ]

    def wait_recv(target, receive):
        remote(target, target, receive, receive, (other, tile)).wait_recv()

    to_core.wait()
    wait_recv(far.at[0], far_sem.at[0])
    wait_recv(far.at[1], far_sem.at[1])

    def across(value):
        return jnp.concatenate([value[:side], value[side:]], axis=1)

    def down(value):
        return jnp.concatenate([value[:, :side], value[:, side:]], axis=0)

    def transmit(t, w_re, w_im):
        return jnp.concatenate(
            [(t[0] * w_re - t[1] * w_im).astype(BF16), (t[0] * w_im + t[1] * w_re).astype(BF16)],
            axis=1,
        )

    def conj_times(a_re, a_im, b_re, b_im):
        return a_re * b_re + a_im * b_im, a_re * b_im - a_im * b_re

    entered = transmit(window(0), psi0[0].astype(F32), psi0[1].astype(F32))
    inner = dot(entered, klt[...]).astype(BF16)
    psi1[...] = dot(kl[...], down(inner)).astype(BF16)
    window1 = window(1)
    entered = transmit(window1, psi1[:side].astype(F32), psi1[side:].astype(F32))
    inner = dot(entered, flct[...]).astype(BF16)
    leave = dot(flr[...], down(inner)).astype(BF16)

    @pl.when(first)
    def _():
        local_intensity.wait()

    @pl.when(jnp.logical_not(first))
    def _():
        wait_recv(measured.at[:half], measured_sem.at[0])
        wait_recv(measured.at[half:], measured_sem.at[1])

    leave_re = leave[:side].astype(F32)
    leave_im = leave[side:].astype(F32)
    factor = 2.0 * (leave_re * leave_re + leave_im * leave_im - measured[...].astype(F32)) * live
    residual = jnp.concatenate(
        [(factor * leave_re).astype(BF16), (factor * leave_im).astype(BF16)], axis=0
    )

    far_tile = jnp.where(first, after, before)
    inner = dot(flrt[...], residual).astype(BF16)
    spread = dot(across(inner), flc[...]).astype(BF16).astype(F32)
    grad_re, grad_im = conj_times(
        psi1[:side].astype(F32), psi1[side:].astype(F32), spread[:, :side], spread[:, side:]
    )
    grad[1, 0] = grad_re.astype(BF16)
    grad[1, 1] = grad_im.astype(BF16)
    grad_to_far1 = remote(
        grad.at[1], grad_far.at[sec], grad_send.at[1], grad_far_sem.at[sec], (1, far_tile)
    )
    grad_to_far1.start()
    next_re, next_im = conj_times(window1[0], window1[1], spread[:, :side], spread[:, side:])
    entering = jnp.concatenate([next_re.astype(BF16), next_im.astype(BF16)], axis=0)
    inner = dot(klt[...], entering).astype(BF16)
    spread = dot(across(inner), kl[...]).astype(BF16).astype(F32)
    grad_re, grad_im = conj_times(
        psi0[0].astype(F32), psi0[1].astype(F32), spread[:, :side], spread[:, side:]
    )
    grad[0, 0] = grad_re.astype(BF16)
    grad[0, 1] = grad_im.astype(BF16)
    grad_to_far0 = remote(
        grad.at[0], grad_far.at[sec], grad_send.at[0], grad_far_sem.at[sec], (0, far_tile)
    )
    grad_to_far0.start()
    grad_to_core = remote(
        grad.at[other], grad_core, grad_core_sem.at[0], grad_core_sem.at[1], (other, tile)
    )
    grad_to_core.start()

    def put(source, here_rows, left_col, gate, start):
        turned = column < left_col
        for part in range(2):
            value = jnp.where(here_rows, source[part].astype(F32), 0.0) * gate
            left = jnp.where(turned, 0.0, value)
            right = jnp.where(turned, value, 0.0)
            if start:
                out_ref[part, 0, :, :side] = left
                out_ref[part, 0, :, side:] = right
            else:
                out_ref[part, 0, :, :side] += left
                out_ref[part, 0, :, side:] += right

    put(grad.at[sec], mine_rows, my_col, jnp.where(edge_second, 0.0, 1.0), True)
    grad_to_core.wait()
    their_rows = (row < their_row) == first
    put(grad_core, their_rows, their_col, jnp.where(first & (tile == 0), 0.0, 1.0), False)
    wait_recv(grad_far.at[0], grad_far_sem.at[0])
    put(
        grad_far.at[0],
        row < prev_vec[0],
        prev_vec[2],
        jnp.where(tile == 0, 0.0, 1.0),
        False,
    )
    wait_recv(grad_far.at[1], grad_far_sem.at[1])
    put(grad_far.at[1], row >= own_vec[1], own_vec[3], 1.0, False)

    to_next.wait_send()
    to_prev.wait_send()
    intensity.wait_send()
    grad_to_far0.wait_send()
    grad_to_far1.wait_send()


def on_device(tiles, object_field, probe, phases, intensities, pos_row, pos_col, counts):
    side = probe.shape[1]
    cosine, sine = angle_tables(side)
    smem = pl.BlockSpec(memory_space=pltpu.SMEM)
    anywhere = pl.BlockSpec(memory_space=pl.ANY)
    block = (2, side, side)
    wide = (2 * side, 2 * side)
    dma = pltpu.SemaphoreType.DMA
    return pl.pallas_call(
        functools.partial(kernel, tiles, side),
        out_shape=jax.ShapeDtypeStruct(object_field.shape, F32),
        in_specs=[smem] * 3 + [anywhere] * 6,
        out_specs=pl.BlockSpec(memory_space=pltpu.VMEM),
        scratch_shapes=[
            pltpu.VMEM((2, side, object_field.shape[3]), BF16),
            pltpu.VMEM(block, BF16),
            pltpu.VMEM((1, side), F32),
            pltpu.VMEM((side, side), F32),
            pltpu.VMEM((side, side), F32),
            pltpu.VMEM((side, side), BF16),
            pltpu.VMEM((8, side), jnp.int32),
            pltpu.VMEM((8, side), jnp.int32),
            pltpu.VMEM(block, BF16),
            pltpu.VMEM(block, BF16),
            pltpu.VMEM(block, BF16),
            pltpu.VMEM((2,) + block, BF16),
            pltpu.VMEM((2,) + block, BF16),
            pltpu.VMEM(wide, BF16),
            pltpu.VMEM(wide, BF16),
            pltpu.VMEM(wide, BF16),
            pltpu.VMEM(wide, BF16),
            pltpu.VMEM(wide, BF16),
            pltpu.VMEM(wide, BF16),
            pltpu.VMEM(block, BF16),
            pltpu.VMEM((2 * side, side), BF16),
            pltpu.VMEM((2,) + block, BF16),
            pltpu.VMEM(block, BF16),
            pltpu.VMEM((2,) + block, BF16),
            dma((6,)),
            dma((2,)),
            dma((2,)),
            dma((1,)),
            dma((1,)),
            dma((2,)),
            dma((1,)),
            dma((2,)),
            dma((2,)),
            dma((2,)),
            dma((2,)),
        ],
        compiler_params=pltpu.CompilerParams(
            collective_id=0, has_side_effects=True, vmem_limit_bytes=48 * 1024 * 1024
        ),
    )(
        pos_row,
        pos_col,
        counts,
        object_field,
        probe,
        phases.reshape(1, side),
        intensities,
        jnp.asarray(cosine),
        jnp.asarray(sine),
    )


def solution(mesh):
    placed = (
        P(None, "sec", "tile", None),
        P(),
        P(),
        P("tile", None, None),
        P("tile"),
        P("tile"),
        P("tile"),
    )
    return jax.shard_map(
        functools.partial(on_device, mesh.shape["tile"]),
        mesh=mesh,
        in_specs=placed,
        out_specs=P(None, "sec", "tile", None),
        check_vma=False,
    )
```

```python
import functools
import math

import jax
import jax.numpy as jnp
import numpy as np
from jax import lax
from jax.experimental import pallas as pl
from jax.experimental.pallas import tpu as pltpu
from jax.sharding import PartitionSpec as P

MESH = pl.DeviceIdType.MESH
F32 = jnp.float32
BF16 = jnp.bfloat16


def dot(a, b):
    return jnp.dot(a, b, preferred_element_type=F32)


def exact_dot(a, b):
    return jnp.dot(a, b, precision=lax.Precision.HIGHEST, preferred_element_type=F32)


def angle_tables(side):
    index = np.arange(side, dtype=np.int64)
    angles = (index[:, None] * index[None, :] % side) * (2.0 * math.pi / side)
    return np.cos(angles).astype(np.float32), np.sin(angles).astype(np.float32)


def kernel(
    tiles,
    side,
    count_ref,
    row_hbm,
    col_hbm,
    object_hbm,
    probe_hbm,
    turn_hbm,
    measured_hbm,
    cosine_hbm,
    sine_hbm,
    out_ref,
    row_ref,
    col_ref,
    field,
    probe,
    turn,
    cosine,
    sine,
    measured,
    mine,
    prev,
    send_core,
    send_next,
    own,
    far,
    kl,
    klt,
    flr,
    flrt,
    flc,
    flct,
    psi0,
    psi1,
    grad,
    grad_core,
    grad_far,
    load_sem,
    scalar_sem,
    core_sem,
    next_sem,
    far_sem,
    measured_sem,
    grad_core_sem,
    grad_send,
    grad_far_sem,
):
    sec = lax.axis_index("sec")
    tile = lax.axis_index("tile")
    other = 1 - sec
    before = lax.rem(tile + tiles - 1, tiles)
    after = lax.rem(tile + 1, tiles)

    loads = [
        pltpu.make_async_copy(row_hbm, row_ref, load_sem.at[0]),
        pltpu.make_async_copy(col_hbm, col_ref, load_sem.at[1]),
        pltpu.make_async_copy(object_hbm.at[:, 0], field, load_sem.at[2]),
        pltpu.make_async_copy(probe_hbm, probe, load_sem.at[3]),
        pltpu.make_async_copy(turn_hbm, turn, load_sem.at[4]),
        pltpu.make_async_copy(cosine_hbm, cosine, load_sem.at[5]),
        pltpu.make_async_copy(sine_hbm, sine, load_sem.at[6]),
    ]
    for load in loads:
        load.start()

    barrier = pltpu.get_barrier_semaphore()
    partners = [(other, tile), (0, before), (1, before)]
    for partner in partners:
        pl.semaphore_signal(barrier, inc=1, device_id=partner, device_id_type=MESH)

    for load in loads[:2]:
        load.wait()
    line = lax.broadcasted_iota(jnp.int32, (8, side), 0)
    values = jnp.zeros((8, side), jnp.int32)
    for at, value in enumerate((row_ref[0], row_ref[1], col_ref[0], col_ref[1], count_ref[0])):
        values = jnp.where(line == at, value, values)
    mine[...] = values

    def remote(source, target, send, receive, device):
        return pltpu.make_async_remote_copy(
            source, target, send, receive, device_id=device, device_id_type=MESH
        )

    first = sec == 0
    column = lax.broadcasted_iota(jnp.int32, (side, side), 1)
    row = lax.broadcasted_iota(jnp.int32, (side, side), 0)

    def pick(target, left_col):
        turned = column < left_col
        for part in range(2):
            target[part] = jnp.where(turned, field[part, :, side:], field[part, :, :side])

    loads[2].wait()
    pick(send_next.at[0], col_ref[0])
    pl.semaphore_wait(barrier, len(partners))
    to_next = [
        remote(send_next.at[slot], far.at[sec], next_sem.at[slot], far_sem.at[sec], (slot, after))
        for slot in range(2)
    ]
    to_next[0].start()
    scalars = remote(mine, prev, scalar_sem.at[0], scalar_sem.at[1], (sec, after))
    scalars.start()
    pick(send_next.at[1], col_ref[1])
    to_next[1].start()
    intensity = remote(
        measured_hbm.at[sec], measured, measured_sem.at[0], measured_sem.at[1], (sec, after)
    )
    intensity.start()

    scalars.wait()
    my_row = jnp.where(first, prev[0:1, :], prev[1:2, :])
    my_col = jnp.where(first, prev[2:3, :], prev[3:4, :])
    their_row = jnp.where(first, prev[1:2, :], prev[0:1, :])
    their_col = jnp.where(first, prev[3:4, :], prev[2:3, :])
    live = (prev[4:5, :] > sec).astype(F32)
    pick(send_core, their_col)
    to_core = remote(send_core, own.at[sec], core_sem.at[0], core_sem.at[1], (other, tile))
    to_core.start()
    pick(own.at[sec], my_col)

    for load in loads[3:]:
        load.wait()
    cos_table = cosine[...]
    sin_table = sine[...]
    phase = turn[...]
    phase_cos = jnp.cos(phase)
    phase_sin = jnp.sin(phase)
    turned_re = cos_table * phase_cos - sin_table * phase_sin
    turned_im = sin_table * phase_cos + cos_table * phase_sin
    scale = 1.0 / side
    k_re = (exact_dot(turned_re, cos_table) + exact_dot(turned_im, sin_table)) * scale
    k_im = (exact_dot(turned_im, cos_table) - exact_dot(turned_re, sin_table)) * scale

    def fill(target, re, im):
        target[:side, :side] = re
        target[:side, side:] = -im
        target[side:, :side] = im
        target[side:, side:] = re

    fill(kl, k_re.astype(BF16), k_im.astype(BF16))
    fill(klt, k_re.T.astype(BF16), -(k_im.T).astype(BF16))

    def one_hot(difference, shift):
        return ((difference & (side - 1)) == (shift & (side - 1))).astype(F32).astype(BF16)

    roll_rows = one_hot(row - column, my_row)
    roll_rows_t = one_hot(column - row, my_row)
    roll_cols = one_hot(row - column, my_col)
    roll_cols_t = one_hot(column - row, my_col)
    norm_scale = 1.0 / math.sqrt(side)
    far_re = (cos_table * norm_scale).astype(BF16)
    far_im = (-sin_table * norm_scale).astype(BF16)
    fill(flr, dot(far_re, roll_rows_t).astype(BF16), dot(far_im, roll_rows_t).astype(BF16))
    fill(flrt, dot(roll_rows, far_re).astype(BF16), -dot(roll_rows, far_im).astype(BF16))
    fill(flc, dot(far_re, roll_cols_t).astype(BF16), dot(far_im, roll_cols_t).astype(BF16))
    fill(flct, dot(roll_cols, far_re).astype(BF16), -dot(roll_cols, far_im).astype(BF16))
    for part in range(2):
        half_way = dot(roll_rows, probe[part]).astype(BF16)
        psi0[part] = dot(half_way, roll_cols_t).astype(BF16)

    in_next = row < my_row
    has_next = jnp.where(tile == 0, 0.0, 1.0)
    own_gate = jnp.where(in_next, has_next, 0.0)
    far_gate = jnp.where(in_next, 0.0, 1.0)

    def window(layer):
        return [
            own[layer, part].astype(F32) * own_gate + far[layer, part].astype(F32) * far_gate
            for part in range(2)
        ]

    def wait_recv(target, receive):
        remote(target, target, receive, receive, (other, tile)).wait_recv()

    to_core.wait()
    wait_recv(far.at[0], far_sem.at[0])
    wait_recv(far.at[1], far_sem.at[1])

    def across(value):
        return jnp.concatenate([value[:side], value[side:]], axis=1)

    def down(value):
        return jnp.concatenate([value[:, :side], value[:, side:]], axis=0)

    def transmit(t, w_re, w_im):
        return jnp.concatenate(
            [(t[0] * w_re - t[1] * w_im).astype(BF16), (t[0] * w_im + t[1] * w_re).astype(BF16)],
            axis=1,
        )

    def conj_times(a_re, a_im, b_re, b_im):
        return a_re * b_re + a_im * b_im, a_re * b_im - a_im * b_re

    entered = transmit(window(0), psi0[0].astype(F32), psi0[1].astype(F32))
    inner = dot(entered, klt[...]).astype(BF16)
    psi1[...] = dot(kl[...], down(inner)).astype(BF16)
    window1 = window(1)
    entered = transmit(window1, psi1[:side].astype(F32), psi1[side:].astype(F32))
    inner = dot(entered, flct[...]).astype(BF16)
    leave = dot(flr[...], down(inner)).astype(BF16)

    intensity.wait_recv()
    leave_re = leave[:side].astype(F32)
    leave_im = leave[side:].astype(F32)
    factor = 2.0 * (leave_re * leave_re + leave_im * leave_im - measured[...].astype(F32)) * live
    residual = jnp.concatenate(
        [(factor * leave_re).astype(BF16), (factor * leave_im).astype(BF16)], axis=0
    )

    inner = dot(flrt[...], residual).astype(BF16)
    spread = dot(across(inner), flc[...]).astype(BF16).astype(F32)
    grad_re, grad_im = conj_times(
        psi1[:side].astype(F32), psi1[side:].astype(F32), spread[:, :side], spread[:, side:]
    )
    grad[1, 0] = grad_re.astype(BF16)
    grad[1, 1] = grad_im.astype(BF16)
    grad_to_far1 = remote(
        grad.at[1], grad_far.at[sec], grad_send.at[1], grad_far_sem.at[sec], (1, before)
    )
    grad_to_far1.start()
    next_re, next_im = conj_times(window1[0], window1[1], spread[:, :side], spread[:, side:])
    entering = jnp.concatenate([next_re.astype(BF16), next_im.astype(BF16)], axis=0)
    inner = dot(klt[...], entering).astype(BF16)
    spread = dot(across(inner), kl[...]).astype(BF16).astype(F32)
    grad_re, grad_im = conj_times(
        psi0[0].astype(F32), psi0[1].astype(F32), spread[:, :side], spread[:, side:]
    )
    grad[0, 0] = grad_re.astype(BF16)
    grad[0, 1] = grad_im.astype(BF16)
    grad_to_far0 = remote(
        grad.at[0], grad_far.at[sec], grad_send.at[0], grad_far_sem.at[sec], (0, before)
    )
    grad_to_far0.start()
    grad_to_core = remote(
        grad.at[other], grad_core, grad_core_sem.at[0], grad_core_sem.at[1], (other, tile)
    )
    grad_to_core.start()

    def put(source, here_rows, left_col, gate, start):
        turned = column < left_col
        for part in range(2):
            value = jnp.where(here_rows, source[part].astype(F32), 0.0) * gate
            left = jnp.where(turned, 0.0, value)
            right = jnp.where(turned, value, 0.0)
            if start:
                out_ref[part, 0, :, :side] = left
                out_ref[part, 0, :, side:] = right
            else:
                out_ref[part, 0, :, :side] += left
                out_ref[part, 0, :, side:] += right

    put(grad.at[sec], in_next, my_col, has_next, True)
    for slot in range(2):
        wait_recv(grad_far.at[slot], grad_far_sem.at[slot])
        put(grad_far.at[slot], row >= row_ref[slot], col_ref[slot], 1.0, False)
    grad_to_core.wait()
    put(grad_core, row < their_row, their_col, has_next, False)

    for sent in to_next:
        sent.wait_send()
    intensity.wait_send()
    grad_to_far0.wait_send()
    grad_to_far1.wait_send()


def on_device(tiles, object_field, probe, phases, intensities, pos_row, pos_col, counts):
    side = probe.shape[1]
    cosine, sine = angle_tables(side)
    anywhere = pl.BlockSpec(memory_space=pltpu.HBM)
    block = (2, side, side)
    wide = (2 * side, 2 * side)
    dma = pltpu.SemaphoreType.DMA
    return pl.pallas_call(
        functools.partial(kernel, tiles, side),
        out_shape=jax.ShapeDtypeStruct(object_field.shape, F32),
        in_specs=[pl.BlockSpec(memory_space=pltpu.SMEM)] + [anywhere] * 8,
        out_specs=pl.BlockSpec(memory_space=pltpu.VMEM),
        scratch_shapes=[
            pltpu.SMEM((2,), jnp.int32),
            pltpu.SMEM((2,), jnp.int32),
            pltpu.VMEM((2, side, object_field.shape[3]), BF16),
            pltpu.VMEM(block, BF16),
            pltpu.VMEM((1, side), F32),
            pltpu.VMEM((side, side), F32),
            pltpu.VMEM((side, side), F32),
            pltpu.VMEM((side, side), BF16),
            pltpu.VMEM((8, side), jnp.int32),
            pltpu.VMEM((8, side), jnp.int32),
            pltpu.VMEM(block, BF16),
            pltpu.VMEM((2,) + block, BF16),
            pltpu.VMEM((2,) + block, BF16),
            pltpu.VMEM((2,) + block, BF16),
            pltpu.VMEM(wide, BF16),
            pltpu.VMEM(wide, BF16),
            pltpu.VMEM(wide, BF16),
            pltpu.VMEM(wide, BF16),
            pltpu.VMEM(wide, BF16),
            pltpu.VMEM(wide, BF16),
            pltpu.VMEM(block, BF16),
            pltpu.VMEM((2 * side, side), BF16),
            pltpu.VMEM((2,) + block, BF16),
            pltpu.VMEM(block, BF16),
            pltpu.VMEM((2,) + block, BF16),
            dma((7,)),
            dma((2,)),
            dma((2,)),
            dma((2,)),
            dma((2,)),
            dma((2,)),
            dma((2,)),
            dma((2,)),
            dma((2,)),
        ],
        compiler_params=pltpu.CompilerParams(
            collective_id=0, has_side_effects=True, vmem_limit_bytes=48 * 1024 * 1024
        ),
    )(
        counts,
        *(
            pltpu.with_memory_space_constraint(value, pltpu.HBM)
            for value in (
                pos_row,
                pos_col,
                object_field,
                probe,
                phases.reshape(1, side),
                intensities,
                jnp.asarray(cosine),
                jnp.asarray(sine),
            )
        )
    )


def solution(mesh):
    placed = (
        P(None, "sec", "tile", None),
        P(),
        P(),
        P("tile", None, None),
        P("tile"),
        P("tile"),
        P("tile"),
    )
    return jax.shard_map(
        functools.partial(on_device, mesh.shape["tile"]),
        mesh=mesh,
        in_specs=placed,
        out_specs=P(None, "sec", "tile", None),
        check_vma=False,
    )
```

```python
import functools
import math

import jax
import jax.numpy as jnp
import numpy as np
from jax import lax
from jax.experimental import pallas as pl
from jax.experimental.pallas import tpu as pltpu
from jax.sharding import PartitionSpec as P

MESH = pl.DeviceIdType.MESH
F32 = jnp.float32
BF16 = jnp.bfloat16


def dot(a, b):
    return jnp.dot(a, b, preferred_element_type=F32)


def exact_dot(a, b):
    return jnp.dot(a, b, precision=lax.Precision.HIGHEST, preferred_element_type=F32)


def angle_tables(side):
    index = np.arange(side, dtype=np.int64)
    angles = (index[:, None] * index[None, :] % side) * (2.0 * math.pi / side)
    return np.cos(angles).astype(np.float32), np.sin(angles).astype(np.float32)


def kernel(
    tiles,
    side,
    count_ref,
    row_hbm,
    col_hbm,
    object_hbm,
    probe_hbm,
    turn_hbm,
    measured_hbm,
    cosine_hbm,
    sine_hbm,
    out_ref,
    row_ref,
    col_ref,
    field,
    probe,
    turn,
    cosine,
    sine,
    measured,
    mine,
    prev,
    up,
    down,
    core_up,
    core_down,
    far_up,
    far_down,
    kl,
    klt,
    flr,
    flrt,
    flc,
    flct,
    psi0,
    psi1,
    grad,
    grad_core,
    load_sem,
    ready_sem,
    scalar_sem,
    core_send,
    core_sem,
    up_send,
    down_send,
    far_up_sem,
    far_down_sem,
    measured_sem,
    grad_send,
    grad_sem,
):
    sec = lax.axis_index("sec")
    tile = lax.axis_index("tile")
    other = 1 - sec
    first = sec == 0
    has_prev = tile > 0
    has_next = tile < tiles - 1
    before = lax.rem(tile + tiles - 1, tiles)
    after = lax.rem(tile + 1, tiles)

    loads = [
        pltpu.make_async_copy(row_hbm, row_ref, load_sem.at[0]),
        pltpu.make_async_copy(col_hbm, col_ref, load_sem.at[1]),
        pltpu.make_async_copy(object_hbm.at[:, 0], field, load_sem.at[2]),
        pltpu.make_async_copy(measured_hbm.at[sec], measured.at[0], load_sem.at[3]),
        pltpu.make_async_copy(probe_hbm, probe, load_sem.at[4]),
        pltpu.make_async_copy(turn_hbm, turn, load_sem.at[5]),
        pltpu.make_async_copy(cosine_hbm, cosine, load_sem.at[6]),
        pltpu.make_async_copy(sine_hbm, sine, load_sem.at[7]),
    ]
    for load in loads:
        load.start()

    def signal(semaphore, device):
        pl.semaphore_signal(semaphore, inc=1, device_id=device, device_id_type=MESH)

    def remote(source, target, send, receive, device):
        return pltpu.make_async_remote_copy(
            source, target, send, receive, device_id=device, device_id_type=MESH
        )

    barrier = pltpu.get_barrier_semaphore()
    signal(barrier, (other, tile))

    @pl.when(has_prev)
    def _():
        signal(barrier, (0, before))
        signal(barrier, (1, before))

    @pl.when(jnp.logical_not(has_prev))
    def _():
        prev[...] = jnp.zeros_like(prev)
        far_up[...] = jnp.zeros_like(far_up)
        measured[1] = jnp.zeros_like(measured[1])

    @pl.when(jnp.logical_not(has_next))
    def _():
        far_down[...] = jnp.zeros_like(far_down)

    for load in loads[:2]:
        load.wait()
    line = lax.broadcasted_iota(jnp.int32, (8, side), 0)
    values = jnp.zeros((8, side), jnp.int32)
    for at, value in enumerate((row_ref[0], row_ref[1], col_ref[0], col_ref[1], count_ref[0])):
        values = jnp.where(line == at, value, values)
    mine[...] = values

    column = lax.broadcasted_iota(jnp.int32, (side, side), 1)
    row = lax.broadcasted_iota(jnp.int32, (side, side), 0)

    def pick(target, left_col):
        turned = column < left_col
        for part in range(2):
            target[part] = jnp.where(turned, field[part, :, side:], field[part, :, :side])

    to_up = [
        remote(up.at[slot], far_up.at[sec], up_send.at[slot], far_up_sem.at[sec], (slot, after))
        for slot in range(2)
    ]
    scalars = remote(mine, prev, scalar_sem.at[0], scalar_sem.at[1], (sec, after))
    intensity = remote(
        measured_hbm.at[sec], measured.at[1], measured_sem.at[0], measured_sem.at[1], (sec, after)
    )
    loads[2].wait()
    pick(up.at[0], col_ref[0])
    pl.semaphore_wait(barrier, jnp.where(has_next, 3, 1))

    @pl.when(has_next)
    def _():
        to_up[0].start()
        scalars.start()
        signal(ready_sem, (other, after))

    pick(up.at[1], col_ref[1])

    @pl.when(has_next)
    def _():
        to_up[1].start()
        intensity.start()

    to_core_up = remote(
        up.at[other], core_up, core_send.at[0], core_sem.at[0], (other, tile)
    )
    to_core_up.start()

    to_down = [
        remote(
            down.at[slot], far_down.at[sec], down_send.at[slot], far_down_sem.at[sec], (slot, before)
        )
        for slot in range(2)
    ]

    @pl.when(has_prev)
    def _():
        scalars.wait_recv()
        pl.semaphore_wait(ready_sem, 1)

    for slot in range(2):
        pick(down.at[slot], prev[2 + slot : 3 + slot, :])

        @pl.when(has_prev)
        def _():
            to_down[slot].start()

    to_core_down = remote(
        down.at[other], core_down, core_send.at[1], core_sem.at[1], (other, tile)
    )
    to_core_down.start()

    def places(values):
        rows = (values[0:1, :], values[1:2, :])
        cols = (values[2:3, :], values[3:4, :])
        live = (values[4:5, :] > sec).astype(F32)
        my = (jnp.where(first, rows[0], rows[1]), jnp.where(first, cols[0], cols[1]))
        their = (jnp.where(first, rows[1], rows[0]), jnp.where(first, cols[1], cols[0]))
        return my, their, live

    here = places(mine)
    there = places(prev)

    for load in loads[3:]:
        load.wait()
    cos_table = cosine[...]
    sin_table = sine[...]
    phase = turn[...]
    phase_cos = jnp.cos(phase)
    phase_sin = jnp.sin(phase)
    turned_re = cos_table * phase_cos - sin_table * phase_sin
    turned_im = sin_table * phase_cos + cos_table * phase_sin
    scale = 1.0 / side
    k_re = (exact_dot(turned_re, cos_table) + exact_dot(turned_im, sin_table)) * scale
    k_im = (exact_dot(turned_im, cos_table) - exact_dot(turned_re, sin_table)) * scale

    def fill(target, re, im):
        target[:side, :side] = re
        target[:side, side:] = -im
        target[side:, :side] = im
        target[side:, side:] = re

    fill(kl, k_re.astype(BF16), k_im.astype(BF16))
    fill(klt, k_re.T.astype(BF16), -(k_im.T).astype(BF16))

    def one_hot(difference, shift):
        return ((difference & (side - 1)) == (shift & (side - 1))).astype(F32).astype(BF16)

    norm_scale = 1.0 / math.sqrt(side)
    far_re = (cos_table * norm_scale).astype(BF16)
    far_im = (-sin_table * norm_scale).astype(BF16)
    for at, (my_row, my_col) in enumerate((here[0], there[0])):
        roll_rows = one_hot(row - column, my_row)
        roll_rows_t = one_hot(column - row, my_row)
        roll_cols = one_hot(row - column, my_col)
        roll_cols_t = one_hot(column - row, my_col)
        fill(flr.at[at], dot(far_re, roll_rows_t).astype(BF16), dot(far_im, roll_rows_t).astype(BF16))
        fill(flrt.at[at], dot(roll_rows, far_re).astype(BF16), -dot(roll_rows, far_im).astype(BF16))
        fill(flc.at[at], dot(far_re, roll_cols_t).astype(BF16), dot(far_im, roll_cols_t).astype(BF16))
        fill(flct.at[at], dot(roll_cols, far_re).astype(BF16), -dot(roll_cols, far_im).astype(BF16))
        for part in range(2):
            half_way = dot(roll_rows, probe[part]).astype(BF16)
            psi0[at, part] = dot(half_way, roll_cols_t).astype(BF16)

    def wait_recv(target, receive):
        remote(target, target, receive, receive, (other, tile)).wait_recv()

    def across(value):
        return jnp.concatenate([value[:side], value[side:]], axis=1)

    def stacked(value):
        return jnp.concatenate([value[:, :side], value[:, side:]], axis=0)

    def transmit(t, w_re, w_im):
        return jnp.concatenate(
            [(t[0] * w_re - t[1] * w_im).astype(BF16), (t[0] * w_im + t[1] * w_re).astype(BF16)],
            axis=1,
        )

    def conj_times(a_re, a_im, b_re, b_im):
        return a_re * b_re + a_im * b_im, a_re * b_im - a_im * b_re

    def run(at, my_row, live, window, wait_measured):
        in_next = row < my_row
        w_re, w_im = psi0[at, 0].astype(F32), psi0[at, 1].astype(F32)
        entered = transmit(window(0, in_next), w_re, w_im)
        inner = dot(entered, klt[...]).astype(BF16)
        psi1[...] = dot(kl[...], stacked(inner)).astype(BF16)
        window1 = window(1, in_next)
        entered = transmit(window1, psi1[:side].astype(F32), psi1[side:].astype(F32))
        inner = dot(entered, flct[at]).astype(BF16)
        leave = dot(flr[at], stacked(inner)).astype(BF16)
        wait_measured()
        leave_re = leave[:side].astype(F32)
        leave_im = leave[side:].astype(F32)
        level = measured[at].astype(F32)
        factor = 2.0 * (leave_re * leave_re + leave_im * leave_im - level) * live
        residual = jnp.concatenate(
            [(factor * leave_re).astype(BF16), (factor * leave_im).astype(BF16)], axis=0
        )
        inner = dot(flrt[at], residual).astype(BF16)
        spread = dot(across(inner), flc[at]).astype(BF16).astype(F32)
        s_re, s_im = spread[:, :side], spread[:, side:]
        grad_re, grad_im = conj_times(
            psi1[:side].astype(F32), psi1[side:].astype(F32), s_re, s_im
        )
        grad[at, 1, 0] = grad_re.astype(BF16)
        grad[at, 1, 1] = grad_im.astype(BF16)
        next_re, next_im = conj_times(window1[0], window1[1], s_re, s_im)
        entering = jnp.concatenate([next_re.astype(BF16), next_im.astype(BF16)], axis=0)
        inner = dot(klt[...], entering).astype(BF16)
        spread = dot(across(inner), kl[...]).astype(BF16).astype(F32)
        grad_re, grad_im = conj_times(w_re, w_im, spread[:, :side], spread[:, side:])
        grad[at, 0, 0] = grad_re.astype(BF16)
        grad[at, 0, 1] = grad_im.astype(BF16)

    def mixed(in_next, next_block, home_block):
        return [
            jnp.where(in_next, next_block[part].astype(F32), home_block[part].astype(F32))
            for part in range(2)
        ]

    def choose(layer, local, received):
        is_local = sec == layer
        return [
            jnp.where(is_local, local[part].astype(F32), received[part].astype(F32))
            for part in range(2)
        ]

    def put(source, here_rows, left_col, start=False):
        turned = column < left_col
        for part in range(2):
            value = jnp.where(here_rows, source[part].astype(F32), 0.0)
            left = jnp.where(turned, 0.0, value)
            right = jnp.where(turned, value, 0.0)
            if start:
                out_ref[part, 0, :, :side] = left
                out_ref[part, 0, :, side:] = right
            else:
                out_ref[part, 0, :, :side] += left
                out_ref[part, 0, :, side:] += right

    to_core_grad = [
        remote(
            grad.at[at, other], grad_core.at[at], grad_send.at[at], grad_sem.at[at], (other, tile)
        )
        for at in range(2)
    ]

    wait_recv(core_up, core_sem.at[0])

    @pl.when(has_next)
    def _():
        wait_recv(far_down.at[0], far_down_sem.at[0])
        wait_recv(far_down.at[1], far_down_sem.at[1])

    (my_row, my_col), (their_row, their_col), live = here
    run(
        0,
        my_row,
        live,
        lambda layer, in_next: mixed(
            in_next, far_down[layer], choose(layer, up[sec], core_up[...])
        ),
        lambda: None,
    )
    to_core_grad[0].start()
    put(grad[0, sec], row >= my_row, my_col, True)

    (prev_row, prev_col), (prev_their_row, prev_their_col), live = there
    wait_recv(core_down, core_sem.at[1])

    @pl.when(has_prev)
    def _():
        wait_recv(far_up.at[0], far_up_sem.at[0])
        wait_recv(far_up.at[1], far_up_sem.at[1])

    def wait_measured():
        @pl.when(has_prev)
        def _():
            intensity.wait_recv()

    run(
        1,
        prev_row,
        live,
        lambda layer, in_next: mixed(
            in_next, choose(layer, down[sec], core_down[...]), far_up[layer]
        ),
        wait_measured,
    )
    to_core_grad[1].start()
    to_core_grad[0].wait_recv()
    put(grad_core[0], row >= their_row, their_col)
    put(grad[1, sec], (row < prev_row) & has_prev, prev_col)
    to_core_grad[1].wait_recv()
    put(grad_core[1], (row < prev_their_row) & has_prev, prev_their_col)

    for sent in (to_core_up, to_core_down, to_core_grad[0], to_core_grad[1]):
        sent.wait_send()

    @pl.when(has_next)
    def _():
        for sent in (to_up[0], to_up[1], scalars, intensity):
            sent.wait_send()

    @pl.when(has_prev)
    def _():
        to_down[0].wait_send()
        to_down[1].wait_send()


def on_device(tiles, object_field, probe, phases, intensities, pos_row, pos_col, counts):
    side = probe.shape[1]
    cosine, sine = angle_tables(side)
    anywhere = pl.BlockSpec(memory_space=pltpu.HBM)
    block = (2, side, side)
    wide = (2 * side, 2 * side)
    dma = pltpu.SemaphoreType.DMA
    return pl.pallas_call(
        functools.partial(kernel, tiles, side),
        out_shape=jax.ShapeDtypeStruct(object_field.shape, F32),
        in_specs=[pl.BlockSpec(memory_space=pltpu.SMEM)] + [anywhere] * 8,
        out_specs=pl.BlockSpec(memory_space=pltpu.VMEM),
        scratch_shapes=[
            pltpu.SMEM((2,), jnp.int32),
            pltpu.SMEM((2,), jnp.int32),
            pltpu.VMEM((2, side, object_field.shape[3]), BF16),
            pltpu.VMEM(block, BF16),
            pltpu.VMEM((1, side), F32),
            pltpu.VMEM((side, side), F32),
            pltpu.VMEM((side, side), F32),
            pltpu.VMEM((2, side, side), BF16),
            pltpu.VMEM((8, side), jnp.int32),
            pltpu.VMEM((8, side), jnp.int32),
            pltpu.VMEM((2,) + block, BF16),
            pltpu.VMEM((2,) + block, BF16),
            pltpu.VMEM(block, BF16),
            pltpu.VMEM(block, BF16),
            pltpu.VMEM((2,) + block, BF16),
            pltpu.VMEM((2,) + block, BF16),
            pltpu.VMEM(wide, BF16),
            pltpu.VMEM(wide, BF16),
            pltpu.VMEM((2,) + wide, BF16),
            pltpu.VMEM((2,) + wide, BF16),
            pltpu.VMEM((2,) + wide, BF16),
            pltpu.VMEM((2,) + wide, BF16),
            pltpu.VMEM((2,) + block, BF16),
            pltpu.VMEM((2 * side, side), BF16),
            pltpu.VMEM((2, 2) + block, BF16),
            pltpu.VMEM((2,) + block, BF16),
            dma((8,)),
            pltpu.SemaphoreType.REGULAR,
            dma((2,)),
            dma((2,)),
            dma((2,)),
            dma((2,)),
            dma((2,)),
            dma((2,)),
            dma((2,)),
            dma((2,)),
            dma((2,)),
            dma((2,)),
        ],
        compiler_params=pltpu.CompilerParams(
            collective_id=0, has_side_effects=True, vmem_limit_bytes=48 * 1024 * 1024
        ),
    )(
        counts,
        *(
            pltpu.with_memory_space_constraint(value, pltpu.HBM)
            for value in (
                pos_row,
                pos_col,
                object_field,
                probe,
                phases.reshape(1, side),
                intensities,
                jnp.asarray(cosine),
                jnp.asarray(sine),
            )
        )
    )


def solution(mesh):
    placed = (
        P(None, "sec", "tile", None),
        P(),
        P(),
        P("tile", None, None),
        P("tile"),
        P("tile"),
        P("tile"),
    )
    return jax.shard_map(
        functools.partial(on_device, mesh.shape["tile"]),
        mesh=mesh,
        in_specs=placed,
        out_specs=P(None, "sec", "tile", None),
        check_vma=False,
    )
```

```python
import functools
import math

import jax
import jax.numpy as jnp
import numpy as np
from jax import lax
from jax.experimental import pallas as pl
from jax.experimental.pallas import tpu as pltpu
from jax.sharding import PartitionSpec as P

MESH = pl.DeviceIdType.MESH
F32 = jnp.float32
BF16 = jnp.bfloat16


def dot(a, b):
    return jnp.dot(a, b, preferred_element_type=F32)


def exact_dot(a, b):
    return jnp.dot(a, b, precision=lax.Precision.HIGHEST, preferred_element_type=F32)


def angle_tables(side):
    index = np.arange(side, dtype=np.int64)
    angles = (index[:, None] * index[None, :] % side) * (2.0 * math.pi / side)
    return np.cos(angles).astype(np.float32), np.sin(angles).astype(np.float32)


def kernel(
    tiles,
    side,
    count_ref,
    row_hbm,
    col_hbm,
    object_hbm,
    probe_hbm,
    turn_hbm,
    measured_hbm,
    cosine_hbm,
    sine_hbm,
    out_ref,
    row_ref,
    col_ref,
    field,
    probe,
    turn,
    cosine,
    sine,
    measured,
    mine,
    prev,
    up,
    down,
    core_up,
    core_down,
    far_up,
    far_down,
    kl,
    klt,
    flr,
    flrt,
    flc,
    flct,
    psi0,
    psi1,
    grad,
    grad_core,
    load_sem,
    ready_sem,
    scalar_sem,
    core_send,
    core_sem,
    up_send,
    down_send,
    far_up_sem,
    far_down_sem,
    measured_send,
    measured_sem,
    grad_send,
    grad_sem,
):
    sec = lax.axis_index("sec")
    tile = lax.axis_index("tile")
    other = 1 - sec
    first = sec == 0
    has_prev = tile > 0
    has_next = tile < tiles - 1
    before = lax.rem(tile + tiles - 1, tiles)
    after = lax.rem(tile + 1, tiles)

    loads = [
        pltpu.make_async_copy(row_hbm, row_ref, load_sem.at[0]),
        pltpu.make_async_copy(col_hbm, col_ref, load_sem.at[1]),
        pltpu.make_async_copy(object_hbm.at[:, 0], field, load_sem.at[2]),
        pltpu.make_async_copy(measured_hbm.at[sec], measured.at[0], load_sem.at[3]),
        pltpu.make_async_copy(probe_hbm, probe, load_sem.at[4]),
        pltpu.make_async_copy(turn_hbm, turn, load_sem.at[5]),
        pltpu.make_async_copy(cosine_hbm, cosine, load_sem.at[6]),
        pltpu.make_async_copy(sine_hbm, sine, load_sem.at[7]),
    ]
    for load in loads:
        load.start()

    def signal(semaphore, device):
        pl.semaphore_signal(semaphore, inc=1, device_id=device, device_id_type=MESH)

    def remote(source, target, send, receive, device):
        return pltpu.make_async_remote_copy(
            source, target, send, receive, device_id=device, device_id_type=MESH
        )

    barrier = pltpu.get_barrier_semaphore()
    signal(barrier, (other, tile))

    @pl.when(has_prev)
    def _():
        signal(barrier, (0, before))
        signal(barrier, (1, before))

    @pl.when(jnp.logical_not(has_prev))
    def _():
        prev[...] = jnp.zeros_like(prev)
        far_up[...] = jnp.zeros_like(far_up)
        measured[1] = jnp.zeros_like(measured[1])

    @pl.when(jnp.logical_not(has_next))
    def _():
        far_down[...] = jnp.zeros_like(far_down)

    column = lax.broadcasted_iota(jnp.int32, (side, side), 1)
    row = lax.broadcasted_iota(jnp.int32, (side, side), 0)

    def pick(target, left_col):
        turned = column < left_col
        for part in range(2):
            target[part] = jnp.where(turned, field[part, :, side:], field[part, :, :side])

    to_up = [
        remote(up.at[slot], far_up.at[sec], up_send.at[slot], far_up_sem.at[sec], (slot, after))
        for slot in range(2)
    ]
    scalars = remote(mine, prev, scalar_sem.at[0], scalar_sem.at[1], (sec, after))
    intensity = [
        remote(
            measured_hbm.at[slot], measured.at[1], measured_send.at[slot], measured_sem, (slot, after)
        )
        for slot in range(2)
    ]
    plane = max(tiles // 4, 3)
    edge = (lax.rem(tile, plane) == 0) | (lax.rem(tile + 1, plane) == 0)
    second = jnp.logical_not(first)
    pl.semaphore_wait(barrier, jnp.where(has_next, 3, 1))

    @pl.when(has_next & second)
    def _():
        intensity[0].start()
        intensity[1].start()

    for load in loads[:2]:
        load.wait()
    line = lax.broadcasted_iota(jnp.int32, (8, side), 0)
    values = jnp.zeros((8, side), jnp.int32)
    for at, value in enumerate((row_ref[0], row_ref[1], col_ref[0], col_ref[1], count_ref[0])):
        values = jnp.where(line == at, value, values)
    mine[...] = values

    @pl.when(has_next)
    def _():
        scalars.start()
        signal(ready_sem, (other, after))

    loads[2].wait()
    for slot in range(2):
        pick(up.at[slot], col_ref[slot])

        @pl.when(has_next & (first | edge))
        def _():
            to_up[slot].start()

    to_core_up = remote(
        up.at[other], core_up, core_send.at[0], core_sem.at[0], (other, tile)
    )

    @pl.when(first | edge)
    def _():
        to_core_up.start()

    to_down = [
        remote(
            down.at[slot], far_down.at[sec], down_send.at[slot], far_down_sem.at[sec], (slot, before)
        )
        for slot in range(2)
    ]

    @pl.when(has_prev)
    def _():
        scalars.wait_recv()
        pl.semaphore_wait(ready_sem, 1)

    for slot in range(2):
        pick(down.at[slot], prev[2 + slot : 3 + slot, :])

        @pl.when(has_prev)
        def _():
            to_down[slot].start()

    @pl.when(second & jnp.logical_not(edge))
    def _():
        to_core_up.start()

        @pl.when(has_next)
        def _():
            to_up[0].start()
            to_up[1].start()

    to_core_down = remote(
        down.at[other], core_down, core_send.at[1], core_sem.at[1], (other, tile)
    )
    to_core_down.start()

    def places(values):
        rows = (values[0:1, :], values[1:2, :])
        cols = (values[2:3, :], values[3:4, :])
        live = (values[4:5, :] > sec).astype(F32)
        my = (jnp.where(first, rows[0], rows[1]), jnp.where(first, cols[0], cols[1]))
        their = (jnp.where(first, rows[1], rows[0]), jnp.where(first, cols[1], cols[0]))
        return my, their, live

    here = places(mine)
    there = places(prev)

    for load in loads[3:]:
        load.wait()
    cos_table = cosine[...]
    sin_table = sine[...]
    phase = turn[...]
    phase_cos = jnp.cos(phase)
    phase_sin = jnp.sin(phase)
    turned_re = cos_table * phase_cos - sin_table * phase_sin
    turned_im = sin_table * phase_cos + cos_table * phase_sin
    scale = 1.0 / side
    k_re = (exact_dot(turned_re, cos_table) + exact_dot(turned_im, sin_table)) * scale
    k_im = (exact_dot(turned_im, cos_table) - exact_dot(turned_re, sin_table)) * scale

    def fill(target, re, im):
        target[:side, :side] = re
        target[:side, side:] = -im
        target[side:, :side] = im
        target[side:, side:] = re

    fill(kl, k_re.astype(BF16), k_im.astype(BF16))
    fill(klt, k_re.T.astype(BF16), -(k_im.T).astype(BF16))

    def one_hot(difference, shift):
        return ((difference & (side - 1)) == (shift & (side - 1))).astype(F32).astype(BF16)

    norm_scale = 1.0 / math.sqrt(side)
    far_re = (cos_table * norm_scale).astype(BF16)
    far_im = (-sin_table * norm_scale).astype(BF16)
    for at, (my_row, my_col) in enumerate((here[0], there[0])):
        roll_rows = one_hot(row - column, my_row)
        roll_rows_t = one_hot(column - row, my_row)
        roll_cols = one_hot(row - column, my_col)
        roll_cols_t = one_hot(column - row, my_col)
        fill(flr.at[at], dot(far_re, roll_rows_t).astype(BF16), dot(far_im, roll_rows_t).astype(BF16))
        fill(flrt.at[at], dot(roll_rows, far_re).astype(BF16), -dot(roll_rows, far_im).astype(BF16))
        fill(flc.at[at], dot(far_re, roll_cols_t).astype(BF16), dot(far_im, roll_cols_t).astype(BF16))
        fill(flct.at[at], dot(roll_cols, far_re).astype(BF16), -dot(roll_cols, far_im).astype(BF16))
        for part in range(2):
            half_way = dot(roll_rows, probe[part]).astype(BF16)
            psi0[at, part] = dot(half_way, roll_cols_t).astype(BF16)

    def wait_recv(target, receive):
        remote(target, target, receive, receive, (other, tile)).wait_recv()

    def across(value):
        return jnp.concatenate([value[:side], value[side:]], axis=1)

    def stacked(value):
        return jnp.concatenate([value[:, :side], value[:, side:]], axis=0)

    def transmit(t, w_re, w_im):
        return jnp.concatenate(
            [(t[0] * w_re - t[1] * w_im).astype(BF16), (t[0] * w_im + t[1] * w_re).astype(BF16)],
            axis=1,
        )

    def conj_times(a_re, a_im, b_re, b_im):
        return a_re * b_re + a_im * b_im, a_re * b_im - a_im * b_re

    to_core_grad = [
        remote(
            grad.at[at, other], grad_core.at[at], grad_send.at[at], grad_sem.at[at], (other, tile)
        )
        for at in range(2)
    ]

    def run(at, my_row, live, window, wait_layer, wait_measured):
        in_next = row < my_row
        w_re, w_im = psi0[at, 0].astype(F32), psi0[at, 1].astype(F32)
        wait_layer(0)
        entered = transmit(window(0, in_next), w_re, w_im)
        inner = dot(entered, klt[...]).astype(BF16)
        psi1[...] = dot(kl[...], stacked(inner)).astype(BF16)
        wait_layer(1)
        window1 = window(1, in_next)
        entered = transmit(window1, psi1[:side].astype(F32), psi1[side:].astype(F32))
        inner = dot(entered, flct[at]).astype(BF16)
        leave = dot(flr[at], stacked(inner)).astype(BF16)
        wait_measured()
        leave_re = leave[:side].astype(F32)
        leave_im = leave[side:].astype(F32)
        level = measured[at].astype(F32)
        factor = 2.0 * (leave_re * leave_re + leave_im * leave_im - level) * live
        residual = jnp.concatenate(
            [(factor * leave_re).astype(BF16), (factor * leave_im).astype(BF16)], axis=0
        )
        inner = dot(flrt[at], residual).astype(BF16)
        spread = dot(across(inner), flc[at]).astype(BF16).astype(F32)
        s_re, s_im = spread[:, :side], spread[:, side:]
        grad_re, grad_im = conj_times(
            psi1[:side].astype(F32), psi1[side:].astype(F32), s_re, s_im
        )
        grad[at, 1, 0] = grad_re.astype(BF16)
        grad[at, 1, 1] = grad_im.astype(BF16)

        @pl.when(first)
        def _():
            to_core_grad[at].start()

        next_re, next_im = conj_times(window1[0], window1[1], s_re, s_im)
        entering = jnp.concatenate([next_re.astype(BF16), next_im.astype(BF16)], axis=0)
        inner = dot(klt[...], entering).astype(BF16)
        spread = dot(across(inner), kl[...]).astype(BF16).astype(F32)
        grad_re, grad_im = conj_times(w_re, w_im, spread[:, :side], spread[:, side:])
        grad[at, 0, 0] = grad_re.astype(BF16)
        grad[at, 0, 1] = grad_im.astype(BF16)

        @pl.when(second)
        def _():
            to_core_grad[at].start()

    def mixed(in_next, next_block, home_block):
        return [
            jnp.where(in_next, next_block[part].astype(F32), home_block[part].astype(F32))
            for part in range(2)
        ]

    def choose(layer, local, received):
        is_local = sec == layer
        return [
            jnp.where(is_local, local[part].astype(F32), received[part].astype(F32))
            for part in range(2)
        ]

    def put(source, here_rows, left_col, start=False):
        turned = column < left_col
        for part in range(2):
            value = jnp.where(here_rows, source[part].astype(F32), 0.0)
            left = jnp.where(turned, 0.0, value)
            right = jnp.where(turned, value, 0.0)
            if start:
                out_ref[part, 0, :, :side] = left
                out_ref[part, 0, :, side:] = right
            else:
                out_ref[part, 0, :, :side] += left
                out_ref[part, 0, :, side:] += right

    wait_recv(core_up, core_sem.at[0])

    def wait_down(layer):
        @pl.when(has_next)
        def _():
            wait_recv(far_down.at[layer], far_down_sem.at[layer])

    (my_row, my_col), (their_row, their_col), live = here
    run(
        0,
        my_row,
        live,
        lambda layer, in_next: mixed(
            in_next, far_down[layer], choose(layer, up[sec], core_up[...])
        ),
        wait_down,
        lambda: None,
    )
    put(grad[0, sec], row >= my_row, my_col, True)

    (prev_row, prev_col), (prev_their_row, prev_their_col), live = there
    wait_recv(core_down, core_sem.at[1])

    def wait_up(layer):
        @pl.when(has_prev)
        def _():
            wait_recv(far_up.at[layer], far_up_sem.at[layer])

    def wait_measured():
        @pl.when(has_prev)
        def _():
            wait_recv(measured.at[1], measured_sem)

    run(
        1,
        prev_row,
        live,
        lambda layer, in_next: mixed(
            in_next, choose(layer, down[sec], core_down[...]), far_up[layer]
        ),
        wait_up,
        wait_measured,
    )
    to_core_grad[0].wait_recv()
    put(grad_core[0], row >= their_row, their_col)
    put(grad[1, sec], (row < prev_row) & has_prev, prev_col)
    to_core_grad[1].wait_recv()
    put(grad_core[1], (row < prev_their_row) & has_prev, prev_their_col)

    for sent in (to_core_up, to_core_down, to_core_grad[0], to_core_grad[1]):
        sent.wait_send()

    @pl.when(has_next)
    def _():
        for sent in (to_up[0], to_up[1], scalars):
            sent.wait_send()

    @pl.when(has_next & second)
    def _():
        intensity[0].wait_send()
        intensity[1].wait_send()

    @pl.when(has_prev)
    def _():
        to_down[0].wait_send()
        to_down[1].wait_send()


def on_device(tiles, object_field, probe, phases, intensities, pos_row, pos_col, counts):
    side = probe.shape[1]
    cosine, sine = angle_tables(side)
    anywhere = pl.BlockSpec(memory_space=pltpu.HBM)
    block = (2, side, side)
    wide = (2 * side, 2 * side)
    dma = pltpu.SemaphoreType.DMA
    return pl.pallas_call(
        functools.partial(kernel, tiles, side),
        out_shape=jax.ShapeDtypeStruct(object_field.shape, F32),
        in_specs=[pl.BlockSpec(memory_space=pltpu.SMEM)] + [anywhere] * 8,
        out_specs=pl.BlockSpec(memory_space=pltpu.VMEM),
        scratch_shapes=[
            pltpu.SMEM((2,), jnp.int32),
            pltpu.SMEM((2,), jnp.int32),
            pltpu.VMEM((2, side, object_field.shape[3]), BF16),
            pltpu.VMEM(block, BF16),
            pltpu.VMEM((1, side), F32),
            pltpu.VMEM((side, side), F32),
            pltpu.VMEM((side, side), F32),
            pltpu.VMEM((2, side, side), BF16),
            pltpu.VMEM((8, side), jnp.int32),
            pltpu.VMEM((8, side), jnp.int32),
            pltpu.VMEM((2,) + block, BF16),
            pltpu.VMEM((2,) + block, BF16),
            pltpu.VMEM(block, BF16),
            pltpu.VMEM(block, BF16),
            pltpu.VMEM((2,) + block, BF16),
            pltpu.VMEM((2,) + block, BF16),
            pltpu.VMEM(wide, BF16),
            pltpu.VMEM(wide, BF16),
            pltpu.VMEM((2,) + wide, BF16),
            pltpu.VMEM((2,) + wide, BF16),
            pltpu.VMEM((2,) + wide, BF16),
            pltpu.VMEM((2,) + wide, BF16),
            pltpu.VMEM((2,) + block, BF16),
            pltpu.VMEM((2 * side, side), BF16),
            pltpu.VMEM((2, 2) + block, BF16),
            pltpu.VMEM((2,) + block, BF16),
            dma((8,)),
            pltpu.SemaphoreType.REGULAR,
            dma((2,)),
            dma((2,)),
            dma((2,)),
            dma((2,)),
            dma((2,)),
            dma((2,)),
            dma((2,)),
            dma((2,)),
            dma,
            dma((2,)),
            dma((2,)),
        ],
        compiler_params=pltpu.CompilerParams(
            collective_id=0, has_side_effects=True, vmem_limit_bytes=48 * 1024 * 1024
        ),
    )(
        counts,
        *(
            pltpu.with_memory_space_constraint(value, pltpu.HBM)
            for value in (
                pos_row,
                pos_col,
                object_field,
                probe,
                phases.reshape(1, side),
                intensities,
                jnp.asarray(cosine),
                jnp.asarray(sine),
            )
        )
    )


def solution(mesh):
    placed = (
        P(None, "sec", "tile", None),
        P(),
        P(),
        P("tile", None, None),
        P("tile"),
        P("tile"),
        P("tile"),
    )
    return jax.shard_map(
        functools.partial(on_device, mesh.shape["tile"]),
        mesh=mesh,
        in_specs=placed,
        out_specs=P(None, "sec", "tile", None),
        check_vma=False,
    )
```

```python
import functools
import math

import jax
import jax.numpy as jnp
import numpy as np
from jax import lax
from jax.experimental import pallas as pl
from jax.experimental.pallas import tpu as pltpu
from jax.sharding import PartitionSpec as P

MESH = pl.DeviceIdType.MESH
F32 = jnp.float32
BF16 = jnp.bfloat16


def dot(a, b):
    return jnp.dot(a, b, preferred_element_type=F32)


def exact_dot(a, b):
    return jnp.dot(a, b, precision=lax.Precision.HIGHEST, preferred_element_type=F32)


def angle_tables(side):
    index = np.arange(side, dtype=np.int64)
    angles = (index[:, None] * index[None, :] % side) * (2.0 * math.pi / side)
    return np.cos(angles).astype(np.float32), np.sin(angles).astype(np.float32)


def kernel(
    tiles,
    side,
    count_ref,
    row_hbm,
    col_hbm,
    object_hbm,
    probe_hbm,
    turn_hbm,
    measured_hbm,
    cosine_hbm,
    sine_hbm,
    out_ref,
    row_ref,
    col_ref,
    field,
    probe,
    turn,
    cosine,
    sine,
    measured,
    mine,
    prev,
    up,
    down,
    core_up,
    core_down,
    far_up,
    far_down,
    kl,
    klt,
    flr,
    flrt,
    flc,
    flct,
    psi0,
    psi1,
    grad,
    grad_core,
    load_sem,
    ready_sem,
    scalar_send,
    scalar_sem,
    core_send,
    core_sem,
    up_send,
    down_send,
    far_up_sem,
    far_down_sem,
    measured_send,
    measured_sem,
    grad_send,
    grad_sem,
):
    sec = lax.axis_index("sec")
    tile = lax.axis_index("tile")
    other = 1 - sec
    first = sec == 0
    has_prev = tile > 0
    has_next = tile < tiles - 1
    before = lax.rem(tile + tiles - 1, tiles)
    after = lax.rem(tile + 1, tiles)

    loads = [
        pltpu.make_async_copy(row_hbm, row_ref, load_sem.at[0]),
        pltpu.make_async_copy(col_hbm, col_ref, load_sem.at[1]),
        pltpu.make_async_copy(object_hbm.at[:, 0], field, load_sem.at[2]),
        pltpu.make_async_copy(measured_hbm.at[sec], measured.at[0], load_sem.at[3]),
        pltpu.make_async_copy(probe_hbm, probe, load_sem.at[4]),
        pltpu.make_async_copy(turn_hbm, turn, load_sem.at[5]),
        pltpu.make_async_copy(cosine_hbm, cosine, load_sem.at[6]),
        pltpu.make_async_copy(sine_hbm, sine, load_sem.at[7]),
    ]
    for load in loads:
        load.start()

    def signal(semaphore, device):
        pl.semaphore_signal(semaphore, inc=1, device_id=device, device_id_type=MESH)

    def remote(source, target, send, receive, device):
        return pltpu.make_async_remote_copy(
            source, target, send, receive, device_id=device, device_id_type=MESH
        )

    barrier = pltpu.get_barrier_semaphore()
    signal(barrier, (other, tile))

    @pl.when(has_prev)
    def _():
        signal(barrier, (0, before))
        signal(barrier, (1, before))

    @pl.when(jnp.logical_not(has_prev))
    def _():
        prev[...] = jnp.zeros_like(prev)
        far_up[...] = jnp.zeros_like(far_up)
        measured[1] = jnp.zeros_like(measured[1])

    @pl.when(jnp.logical_not(has_next))
    def _():
        far_down[...] = jnp.zeros_like(far_down)

    column = lax.broadcasted_iota(jnp.int32, (side, side), 1)
    row = lax.broadcasted_iota(jnp.int32, (side, side), 0)

    def pick(target, left_col):
        turned = column < left_col
        for part in range(2):
            target[part] = jnp.where(turned, field[part, :, side:], field[part, :, :side])

    to_up = [
        remote(up.at[slot], far_up.at[sec], up_send.at[slot], far_up_sem.at[sec], (slot, after))
        for slot in range(2)
    ]
    scalars = [
        remote(mine, prev, scalar_send.at[slot], scalar_sem, (slot, after)) for slot in range(2)
    ]
    intensity = [
        remote(
            measured_hbm.at[slot], measured.at[1], measured_send.at[slot], measured_sem, (slot, after)
        )
        for slot in range(2)
    ]
    plane = max(tiles // 4, 3)
    edge = (lax.rem(tile, plane) == 0) | (lax.rem(tile + 1, plane) == 0)
    second = jnp.logical_not(first)
    pl.semaphore_wait(barrier, jnp.where(has_next, 3, 1))

    @pl.when(has_next & second)
    def _():
        signal(ready_sem, (0, after))
        signal(ready_sem, (1, after))
        intensity[0].start()

    for load in loads[:2]:
        load.wait()
    line = lax.broadcasted_iota(jnp.int32, (8, side), 0)
    values = jnp.zeros((8, side), jnp.int32)
    for at, value in enumerate((row_ref[0], row_ref[1], col_ref[0], col_ref[1], count_ref[0])):
        values = jnp.where(line == at, value, values)
    mine[...] = values

    @pl.when(has_next & first)
    def _():
        scalars[0].start()
        scalars[1].start()

    loads[2].wait()
    for slot in range(2):
        pick(up.at[slot], col_ref[slot])

        @pl.when(has_next & (first | edge))
        def _():
            to_up[slot].start()

    @pl.when(has_next & second & edge)
    def _():
        intensity[1].start()

    to_core_up = remote(
        up.at[other], core_up, core_send.at[0], core_sem.at[0], (other, tile)
    )

    @pl.when(first | edge)
    def _():
        to_core_up.start()

    to_down = [
        remote(
            down.at[slot], far_down.at[sec], down_send.at[slot], far_down_sem.at[sec], (slot, before)
        )
        for slot in range(2)
    ]

    @pl.when(has_prev)
    def _():
        remote(prev, prev, scalar_sem, scalar_sem, (other, tile)).wait_recv()
        pl.semaphore_wait(ready_sem, 1)

    for slot in range(2):
        pick(down.at[slot], prev[2 + slot : 3 + slot, :])

        @pl.when(has_prev)
        def _():
            to_down[slot].start()

    @pl.when(second & jnp.logical_not(edge))
    def _():
        to_core_up.start()

        @pl.when(has_next)
        def _():
            to_up[0].start()
            to_up[1].start()
            intensity[1].start()

    to_core_down = remote(
        down.at[other], core_down, core_send.at[1], core_sem.at[1], (other, tile)
    )
    to_core_down.start()

    def places(values):
        rows = (values[0:1, :], values[1:2, :])
        cols = (values[2:3, :], values[3:4, :])
        live = (values[4:5, :] > sec).astype(F32)
        my = (jnp.where(first, rows[0], rows[1]), jnp.where(first, cols[0], cols[1]))
        their = (jnp.where(first, rows[1], rows[0]), jnp.where(first, cols[1], cols[0]))
        return my, their, live

    here = places(mine)
    there = places(prev)

    for load in loads[3:]:
        load.wait()
    cos_table = cosine[...]
    sin_table = sine[...]
    phase = turn[...]
    phase_cos = jnp.cos(phase)
    phase_sin = jnp.sin(phase)
    turned_re = cos_table * phase_cos - sin_table * phase_sin
    turned_im = sin_table * phase_cos + cos_table * phase_sin
    scale = 1.0 / side
    k_re = (exact_dot(turned_re, cos_table) + exact_dot(turned_im, sin_table)) * scale
    k_im = (exact_dot(turned_im, cos_table) - exact_dot(turned_re, sin_table)) * scale

    def fill(target, re, im):
        target[:side, :side] = re
        target[:side, side:] = -im
        target[side:, :side] = im
        target[side:, side:] = re

    fill(kl, k_re.astype(BF16), k_im.astype(BF16))
    fill(klt, k_re.T.astype(BF16), -(k_im.T).astype(BF16))

    def one_hot(difference, shift):
        return ((difference & (side - 1)) == (shift & (side - 1))).astype(F32).astype(BF16)

    norm_scale = 1.0 / math.sqrt(side)
    far_re = (cos_table * norm_scale).astype(BF16)
    far_im = (-sin_table * norm_scale).astype(BF16)
    for at, (my_row, my_col) in enumerate((here[0], there[0])):
        roll_rows = one_hot(row - column, my_row)
        roll_rows_t = one_hot(column - row, my_row)
        roll_cols = one_hot(row - column, my_col)
        roll_cols_t = one_hot(column - row, my_col)
        fill(flr.at[at], dot(far_re, roll_rows_t).astype(BF16), dot(far_im, roll_rows_t).astype(BF16))
        fill(flrt.at[at], dot(roll_rows, far_re).astype(BF16), -dot(roll_rows, far_im).astype(BF16))
        fill(flc.at[at], dot(far_re, roll_cols_t).astype(BF16), dot(far_im, roll_cols_t).astype(BF16))
        fill(flct.at[at], dot(roll_cols, far_re).astype(BF16), -dot(roll_cols, far_im).astype(BF16))
        for part in range(2):
            half_way = dot(roll_rows, probe[part]).astype(BF16)
            psi0[at, part] = dot(half_way, roll_cols_t).astype(BF16)

    def wait_recv(target, receive):
        remote(target, target, receive, receive, (other, tile)).wait_recv()

    def across(value):
        return jnp.concatenate([value[:side], value[side:]], axis=1)

    def stacked(value):
        return jnp.concatenate([value[:, :side], value[:, side:]], axis=0)

    def transmit(t, w_re, w_im):
        return jnp.concatenate(
            [(t[0] * w_re - t[1] * w_im).astype(BF16), (t[0] * w_im + t[1] * w_re).astype(BF16)],
            axis=1,
        )

    def conj_times(a_re, a_im, b_re, b_im):
        return a_re * b_re + a_im * b_im, a_re * b_im - a_im * b_re

    to_core_grad = [
        remote(
            grad.at[at, other], grad_core.at[at], grad_send.at[at], grad_sem.at[at], (other, tile)
        )
        for at in range(2)
    ]

    def run(at, my_row, live, window, wait_layer, wait_measured):
        in_next = row < my_row
        w_re, w_im = psi0[at, 0].astype(F32), psi0[at, 1].astype(F32)
        wait_layer(0)
        entered = transmit(window(0, in_next), w_re, w_im)
        inner = dot(entered, klt[...]).astype(BF16)
        psi1[...] = dot(kl[...], stacked(inner)).astype(BF16)
        wait_layer(1)
        window1 = window(1, in_next)
        entered = transmit(window1, psi1[:side].astype(F32), psi1[side:].astype(F32))
        inner = dot(entered, flct[at]).astype(BF16)
        leave = dot(flr[at], stacked(inner)).astype(BF16)
        wait_measured()
        leave_re = leave[:side].astype(F32)
        leave_im = leave[side:].astype(F32)
        level = measured[at].astype(F32)
        factor = 2.0 * (leave_re * leave_re + leave_im * leave_im - level) * live
        residual = jnp.concatenate(
            [(factor * leave_re).astype(BF16), (factor * leave_im).astype(BF16)], axis=0
        )
        inner = dot(flrt[at], residual).astype(BF16)
        spread = dot(across(inner), flc[at]).astype(BF16).astype(F32)
        s_re, s_im = spread[:, :side], spread[:, side:]
        grad_re, grad_im = conj_times(
            psi1[:side].astype(F32), psi1[side:].astype(F32), s_re, s_im
        )
        grad[at, 1, 0] = grad_re.astype(BF16)
        grad[at, 1, 1] = grad_im.astype(BF16)

        @pl.when(first)
        def _():
            to_core_grad[at].start()

        next_re, next_im = conj_times(window1[0], window1[1], s_re, s_im)
        entering = jnp.concatenate([next_re.astype(BF16), next_im.astype(BF16)], axis=0)
        inner = dot(klt[...], entering).astype(BF16)
        spread = dot(across(inner), kl[...]).astype(BF16).astype(F32)
        grad_re, grad_im = conj_times(w_re, w_im, spread[:, :side], spread[:, side:])
        grad[at, 0, 0] = grad_re.astype(BF16)
        grad[at, 0, 1] = grad_im.astype(BF16)

        @pl.when(second)
        def _():
            to_core_grad[at].start()

    def mixed(in_next, next_block, home_block):
        return [
            jnp.where(in_next, next_block[part].astype(F32), home_block[part].astype(F32))
            for part in range(2)
        ]

    def choose(layer, local, received):
        is_local = sec == layer
        return [
            jnp.where(is_local, local[part].astype(F32), received[part].astype(F32))
            for part in range(2)
        ]

    def put(source, here_rows, left_col, start=False):
        turned = column < left_col
        for part in range(2):
            value = jnp.where(here_rows, source[part].astype(F32), 0.0)
            left = jnp.where(turned, 0.0, value)
            right = jnp.where(turned, value, 0.0)
            if start:
                out_ref[part, 0, :, :side] = left
                out_ref[part, 0, :, side:] = right
            else:
                out_ref[part, 0, :, :side] += left
                out_ref[part, 0, :, side:] += right

    wait_recv(core_up, core_sem.at[0])

    def wait_down(layer):
        @pl.when(has_next)
        def _():
            wait_recv(far_down.at[layer], far_down_sem.at[layer])

    (my_row, my_col), (their_row, their_col), live = here
    run(
        0,
        my_row,
        live,
        lambda layer, in_next: mixed(
            in_next, far_down[layer], choose(layer, up[sec], core_up[...])
        ),
        wait_down,
        lambda: None,
    )
    put(grad[0, sec], row >= my_row, my_col, True)

    (prev_row, prev_col), (prev_their_row, prev_their_col), live = there
    wait_recv(core_down, core_sem.at[1])

    def wait_up(layer):
        @pl.when(has_prev)
        def _():
            wait_recv(far_up.at[layer], far_up_sem.at[layer])

    def wait_measured():
        @pl.when(has_prev)
        def _():
            wait_recv(measured.at[1], measured_sem)

    run(
        1,
        prev_row,
        live,
        lambda layer, in_next: mixed(
            in_next, choose(layer, down[sec], core_down[...]), far_up[layer]
        ),
        wait_up,
        wait_measured,
    )
    to_core_grad[0].wait_recv()
    put(grad_core[0], row >= their_row, their_col)
    put(grad[1, sec], (row < prev_row) & has_prev, prev_col)
    to_core_grad[1].wait_recv()
    put(grad_core[1], (row < prev_their_row) & has_prev, prev_their_col)

    for sent in (to_core_up, to_core_down, to_core_grad[0], to_core_grad[1]):
        sent.wait_send()

    @pl.when(has_next)
    def _():
        to_up[0].wait_send()
        to_up[1].wait_send()

    @pl.when(has_next & first)
    def _():
        scalars[0].wait_send()
        scalars[1].wait_send()

    @pl.when(has_next & second)
    def _():
        intensity[0].wait_send()
        intensity[1].wait_send()

    @pl.when(has_prev)
    def _():
        to_down[0].wait_send()
        to_down[1].wait_send()


def on_device(tiles, object_field, probe, phases, intensities, pos_row, pos_col, counts):
    side = probe.shape[1]
    cosine, sine = angle_tables(side)
    anywhere = pl.BlockSpec(memory_space=pltpu.HBM)
    block = (2, side, side)
    wide = (2 * side, 2 * side)
    dma = pltpu.SemaphoreType.DMA
    return pl.pallas_call(
        functools.partial(kernel, tiles, side),
        out_shape=jax.ShapeDtypeStruct(object_field.shape, F32),
        in_specs=[pl.BlockSpec(memory_space=pltpu.SMEM)] + [anywhere] * 8,
        out_specs=pl.BlockSpec(memory_space=pltpu.VMEM),
        scratch_shapes=[
            pltpu.SMEM((2,), jnp.int32),
            pltpu.SMEM((2,), jnp.int32),
            pltpu.VMEM((2, side, object_field.shape[3]), BF16),
            pltpu.VMEM(block, BF16),
            pltpu.VMEM((1, side), F32),
            pltpu.VMEM((side, side), F32),
            pltpu.VMEM((side, side), F32),
            pltpu.VMEM((2, side, side), BF16),
            pltpu.VMEM((8, side), jnp.int32),
            pltpu.VMEM((8, side), jnp.int32),
            pltpu.VMEM((2,) + block, BF16),
            pltpu.VMEM((2,) + block, BF16),
            pltpu.VMEM(block, BF16),
            pltpu.VMEM(block, BF16),
            pltpu.VMEM((2,) + block, BF16),
            pltpu.VMEM((2,) + block, BF16),
            pltpu.VMEM(wide, BF16),
            pltpu.VMEM(wide, BF16),
            pltpu.VMEM((2,) + wide, BF16),
            pltpu.VMEM((2,) + wide, BF16),
            pltpu.VMEM((2,) + wide, BF16),
            pltpu.VMEM((2,) + wide, BF16),
            pltpu.VMEM((2,) + block, BF16),
            pltpu.VMEM((2 * side, side), BF16),
            pltpu.VMEM((2, 2) + block, BF16),
            pltpu.VMEM((2,) + block, BF16),
            dma((8,)),
            pltpu.SemaphoreType.REGULAR,
            dma((2,)),
            dma,
            dma((2,)),
            dma((2,)),
            dma((2,)),
            dma((2,)),
            dma((2,)),
            dma((2,)),
            dma((2,)),
            dma,
            dma((2,)),
            dma((2,)),
        ],
        compiler_params=pltpu.CompilerParams(
            collective_id=0, has_side_effects=True, vmem_limit_bytes=48 * 1024 * 1024
        ),
    )(
        counts,
        *(
            pltpu.with_memory_space_constraint(value, pltpu.HBM)
            for value in (
                pos_row,
                pos_col,
                object_field,
                probe,
                phases.reshape(1, side),
                intensities,
                jnp.asarray(cosine),
                jnp.asarray(sine),
            )
        )
    )


def solution(mesh):
    placed = (
        P(None, "sec", "tile", None),
        P(),
        P(),
        P("tile", None, None),
        P("tile"),
        P("tile"),
        P("tile"),
    )
    return jax.shard_map(
        functools.partial(on_device, mesh.shape["tile"]),
        mesh=mesh,
        in_specs=placed,
        out_specs=P(None, "sec", "tile", None),
        check_vma=False,
    )
```

```python
import functools
import math

import jax
import jax.numpy as jnp
import numpy as np
from jax import lax
from jax.experimental import pallas as pl
from jax.experimental.pallas import tpu as pltpu
from jax.sharding import PartitionSpec as P

MESH = pl.DeviceIdType.MESH
F32 = jnp.float32
BF16 = jnp.bfloat16


def dot(a, b):
    return jnp.dot(a, b, preferred_element_type=F32)


def exact_dot(a, b):
    return jnp.dot(a, b, precision=lax.Precision.HIGHEST, preferred_element_type=F32)


def angle_tables(side):
    index = np.arange(side, dtype=np.int64)
    angles = (index[:, None] * index[None, :] % side) * (2.0 * math.pi / side)
    return np.cos(angles).astype(np.float32), np.sin(angles).astype(np.float32)


def kernel(
    tiles,
    side,
    count_ref,
    row_hbm,
    col_hbm,
    object_hbm,
    probe_hbm,
    turn_hbm,
    measured_hbm,
    cosine_hbm,
    sine_hbm,
    out_ref,
    row_ref,
    col_ref,
    field,
    probe,
    turn,
    cosine,
    sine,
    measured,
    mine,
    prev,
    up,
    down,
    core_up,
    core_down,
    far_up,
    far_down,
    kl,
    klt,
    flr,
    flrt,
    flc,
    flct,
    psi0,
    psi1,
    grad,
    grad_core,
    load_sem,
    ready_sem,
    scalar_send,
    scalar_sem,
    core_send,
    core_sem,
    up_send,
    down_send,
    far_up_sem,
    far_down_sem,
    measured_send,
    measured_sem,
    grad_send,
    grad_sem,
):
    sec = lax.axis_index("sec")
    tile = lax.axis_index("tile")
    other = 1 - sec
    first = sec == 0
    has_prev = tile > 0
    has_next = tile < tiles - 1
    before = lax.rem(tile + tiles - 1, tiles)
    after = lax.rem(tile + 1, tiles)

    loads = [
        pltpu.make_async_copy(row_hbm, row_ref, load_sem.at[0]),
        pltpu.make_async_copy(col_hbm, col_ref, load_sem.at[1]),
        pltpu.make_async_copy(object_hbm.at[:, 0], field, load_sem.at[2]),
        pltpu.make_async_copy(measured_hbm.at[sec], measured.at[0], load_sem.at[3]),
        pltpu.make_async_copy(probe_hbm, probe, load_sem.at[4]),
        pltpu.make_async_copy(turn_hbm, turn, load_sem.at[5]),
        pltpu.make_async_copy(cosine_hbm, cosine, load_sem.at[6]),
        pltpu.make_async_copy(sine_hbm, sine, load_sem.at[7]),
    ]
    for load in loads:
        load.start()

    def signal(semaphore, device):
        pl.semaphore_signal(semaphore, inc=1, device_id=device, device_id_type=MESH)

    def remote(source, target, send, receive, device):
        return pltpu.make_async_remote_copy(
            source, target, send, receive, device_id=device, device_id_type=MESH
        )

    barrier = pltpu.get_barrier_semaphore()
    signal(barrier, (other, tile))

    @pl.when(has_prev)
    def _():
        signal(barrier, (0, before))
        signal(barrier, (1, before))

    @pl.when(jnp.logical_not(has_prev))
    def _():
        prev[...] = jnp.zeros_like(prev)
        far_up[...] = jnp.zeros_like(far_up)
        measured[1] = jnp.zeros_like(measured[1])

    @pl.when(jnp.logical_not(has_next))
    def _():
        far_down[...] = jnp.zeros_like(far_down)

    column = lax.broadcasted_iota(jnp.int32, (side, side), 1)
    row = lax.broadcasted_iota(jnp.int32, (side, side), 0)

    def pick(target, left_col):
        turned = column < left_col
        for part in range(2):
            target[part] = jnp.where(turned, field[part, :, side:], field[part, :, :side])

    to_up = [
        remote(up.at[slot], far_up.at[sec], up_send.at[slot], far_up_sem.at[sec], (slot, after))
        for slot in range(2)
    ]
    scalars = [
        remote(mine, prev, scalar_send.at[slot], scalar_sem, (slot, after)) for slot in range(2)
    ]
    intensity = [
        remote(
            measured_hbm.at[slot], measured.at[1], measured_send.at[slot], measured_sem, (slot, after)
        )
        for slot in range(2)
    ]
    plane = max(tiles // 4, 3)
    edge = (lax.rem(tile, plane) == 0) | (lax.rem(tile + 1, plane) == 0)
    second = jnp.logical_not(first)
    pl.semaphore_wait(barrier, jnp.where(has_next, 3, 1))

    @pl.when(has_next & second)
    def _():
        signal(ready_sem, (0, after))
        signal(ready_sem, (1, after))
        intensity[0].start()

    for load in loads[:2]:
        load.wait()
    line = lax.broadcasted_iota(jnp.int32, (8, side), 0)
    values = jnp.zeros((8, side), jnp.int32)
    for at, value in enumerate((row_ref[0], row_ref[1], col_ref[0], col_ref[1], count_ref[0])):
        values = jnp.where(line == at, value, values)
    mine[...] = values

    @pl.when(has_next & first)
    def _():
        scalars[0].start()
        scalars[1].start()

    loads[2].wait()
    for slot in range(2):
        pick(up.at[slot], col_ref[slot])

        @pl.when(has_next & (first | edge))
        def _():
            to_up[slot].start()

    @pl.when(has_next & second & edge)
    def _():
        intensity[1].start()

    to_core_up = remote(
        up.at[other], core_up, core_send.at[0], core_sem.at[0], (other, tile)
    )

    @pl.when(first | edge)
    def _():
        to_core_up.start()

    to_down = [
        remote(
            down.at[slot], far_down.at[sec], down_send.at[slot], far_down_sem.at[sec], (slot, before)
        )
        for slot in range(2)
    ]

    @pl.when(has_prev)
    def _():
        remote(prev, prev, scalar_sem, scalar_sem, (other, tile)).wait_recv()
        pl.semaphore_wait(ready_sem, 1)

    for slot in range(2):
        pick(down.at[slot], prev[2 + slot : 3 + slot, :])
    to_core_down = remote(
        down.at[other], core_down, core_send.at[1], core_sem.at[1], (other, tile)
    )
    to_core_down.start()

    @pl.when(has_prev)
    def _():
        to_down[0].start()
        to_down[1].start()

    @pl.when(second & jnp.logical_not(edge))
    def _():
        to_core_up.start()

        @pl.when(has_next)
        def _():
            to_up[0].start()
            to_up[1].start()
            intensity[1].start()

    def places(values):
        rows = (values[0:1, :], values[1:2, :])
        cols = (values[2:3, :], values[3:4, :])
        live = (values[4:5, :] > sec).astype(F32)
        my = (jnp.where(first, rows[0], rows[1]), jnp.where(first, cols[0], cols[1]))
        their = (jnp.where(first, rows[1], rows[0]), jnp.where(first, cols[1], cols[0]))
        return my, their, live

    here = places(mine)
    there = places(prev)

    for load in loads[3:]:
        load.wait()
    cos_table = cosine[...]
    sin_table = sine[...]
    phase = turn[...]
    phase_cos = jnp.cos(phase)
    phase_sin = jnp.sin(phase)
    turned_re = cos_table * phase_cos - sin_table * phase_sin
    turned_im = sin_table * phase_cos + cos_table * phase_sin
    scale = 1.0 / side
    k_re = (exact_dot(turned_re, cos_table) + exact_dot(turned_im, sin_table)) * scale
    k_im = (exact_dot(turned_im, cos_table) - exact_dot(turned_re, sin_table)) * scale

    def fill(target, re, im):
        target[:side, :side] = re
        target[:side, side:] = -im
        target[side:, :side] = im
        target[side:, side:] = re

    fill(kl, k_re.astype(BF16), k_im.astype(BF16))
    fill(klt, k_re.T.astype(BF16), -(k_im.T).astype(BF16))

    def one_hot(difference, shift):
        return ((difference & (side - 1)) == (shift & (side - 1))).astype(F32).astype(BF16)

    norm_scale = 1.0 / math.sqrt(side)
    far_re = (cos_table * norm_scale).astype(BF16)
    far_im = (-sin_table * norm_scale).astype(BF16)
    for at, (my_row, my_col) in enumerate((here[0], there[0])):
        roll_rows = one_hot(row - column, my_row)
        roll_rows_t = one_hot(column - row, my_row)
        roll_cols = one_hot(row - column, my_col)
        roll_cols_t = one_hot(column - row, my_col)
        fill(flr.at[at], dot(far_re, roll_rows_t).astype(BF16), dot(far_im, roll_rows_t).astype(BF16))
        fill(flrt.at[at], dot(roll_rows, far_re).astype(BF16), -dot(roll_rows, far_im).astype(BF16))
        fill(flc.at[at], dot(far_re, roll_cols_t).astype(BF16), dot(far_im, roll_cols_t).astype(BF16))
        fill(flct.at[at], dot(roll_cols, far_re).astype(BF16), -dot(roll_cols, far_im).astype(BF16))
        for part in range(2):
            half_way = dot(roll_rows, probe[part]).astype(BF16)
            psi0[at, part] = dot(half_way, roll_cols_t).astype(BF16)

    def wait_recv(target, receive):
        remote(target, target, receive, receive, (other, tile)).wait_recv()

    def across(value):
        return jnp.concatenate([value[:side], value[side:]], axis=1)

    def stacked(value):
        return jnp.concatenate([value[:, :side], value[:, side:]], axis=0)

    def transmit(t, w_re, w_im):
        return jnp.concatenate(
            [(t[0] * w_re - t[1] * w_im).astype(BF16), (t[0] * w_im + t[1] * w_re).astype(BF16)],
            axis=1,
        )

    def conj_times(a_re, a_im, b_re, b_im):
        return a_re * b_re + a_im * b_im, a_re * b_im - a_im * b_re

    to_core_grad = [
        remote(
            grad.at[at, other], grad_core.at[at], grad_send.at[at], grad_sem.at[at], (other, tile)
        )
        for at in range(2)
    ]

    def run(at, my_row, live, window, wait_layer, wait_measured):
        in_next = row < my_row
        w_re, w_im = psi0[at, 0].astype(F32), psi0[at, 1].astype(F32)
        wait_layer(0)
        entered = transmit(window(0, in_next), w_re, w_im)
        inner = dot(entered, klt[...]).astype(BF16)
        psi1[...] = dot(kl[...], stacked(inner)).astype(BF16)
        wait_layer(1)
        window1 = window(1, in_next)
        entered = transmit(window1, psi1[:side].astype(F32), psi1[side:].astype(F32))
        inner = dot(entered, flct[at]).astype(BF16)
        leave = dot(flr[at], stacked(inner)).astype(BF16)
        wait_measured()
        leave_re = leave[:side].astype(F32)
        leave_im = leave[side:].astype(F32)
        level = measured[at].astype(F32)
        factor = 2.0 * (leave_re * leave_re + leave_im * leave_im - level) * live
        residual = jnp.concatenate(
            [(factor * leave_re).astype(BF16), (factor * leave_im).astype(BF16)], axis=0
        )
        inner = dot(flrt[at], residual).astype(BF16)
        spread = dot(across(inner), flc[at]).astype(BF16).astype(F32)
        s_re, s_im = spread[:, :side], spread[:, side:]
        grad_re, grad_im = conj_times(
            psi1[:side].astype(F32), psi1[side:].astype(F32), s_re, s_im
        )
        grad[at, 1, 0] = grad_re.astype(BF16)
        grad[at, 1, 1] = grad_im.astype(BF16)

        @pl.when(first)
        def _():
            to_core_grad[at].start()

        next_re, next_im = conj_times(window1[0], window1[1], s_re, s_im)
        entering = jnp.concatenate([next_re.astype(BF16), next_im.astype(BF16)], axis=0)
        inner = dot(klt[...], entering).astype(BF16)
        spread = dot(across(inner), kl[...]).astype(BF16).astype(F32)
        grad_re, grad_im = conj_times(w_re, w_im, spread[:, :side], spread[:, side:])
        grad[at, 0, 0] = grad_re.astype(BF16)
        grad[at, 0, 1] = grad_im.astype(BF16)

        @pl.when(second)
        def _():
            to_core_grad[at].start()

    def mixed(in_next, next_block, home_block):
        return [
            jnp.where(in_next, next_block[part].astype(F32), home_block[part].astype(F32))
            for part in range(2)
        ]

    def choose(layer, local, received):
        is_local = sec == layer
        return [
            jnp.where(is_local, local[part].astype(F32), received[part].astype(F32))
            for part in range(2)
        ]

    def put(source, here_rows, left_col, start=False):
        turned = column < left_col
        for part in range(2):
            value = jnp.where(here_rows, source[part].astype(F32), 0.0)
            left = jnp.where(turned, 0.0, value)
            right = jnp.where(turned, value, 0.0)
            if start:
                out_ref[part, 0, :, :side] = left
                out_ref[part, 0, :, side:] = right
            else:
                out_ref[part, 0, :, :side] += left
                out_ref[part, 0, :, side:] += right

    wait_recv(core_up, core_sem.at[0])

    def wait_down(layer):
        @pl.when(has_next)
        def _():
            wait_recv(far_down.at[layer], far_down_sem.at[layer])

    (my_row, my_col), (their_row, their_col), live = here
    run(
        0,
        my_row,
        live,
        lambda layer, in_next: mixed(
            in_next, far_down[layer], choose(layer, up[sec], core_up[...])
        ),
        wait_down,
        lambda: None,
    )
    put(grad[0, sec], row >= my_row, my_col, True)

    (prev_row, prev_col), (prev_their_row, prev_their_col), live = there
    wait_recv(core_down, core_sem.at[1])

    def wait_up(layer):
        @pl.when(has_prev)
        def _():
            wait_recv(far_up.at[layer], far_up_sem.at[layer])

    def wait_measured():
        @pl.when(has_prev)
        def _():
            wait_recv(measured.at[1], measured_sem)

    run(
        1,
        prev_row,
        live,
        lambda layer, in_next: mixed(
            in_next, choose(layer, down[sec], core_down[...]), far_up[layer]
        ),
        wait_up,
        wait_measured,
    )
    to_core_grad[0].wait_recv()
    put(grad_core[0], row >= their_row, their_col)
    put(grad[1, sec], (row < prev_row) & has_prev, prev_col)
    to_core_grad[1].wait_recv()
    put(grad_core[1], (row < prev_their_row) & has_prev, prev_their_col)

    for sent in (to_core_up, to_core_down, to_core_grad[0], to_core_grad[1]):
        sent.wait_send()

    @pl.when(has_next)
    def _():
        to_up[0].wait_send()
        to_up[1].wait_send()

    @pl.when(has_next & first)
    def _():
        scalars[0].wait_send()
        scalars[1].wait_send()

    @pl.when(has_next & second)
    def _():
        intensity[0].wait_send()
        intensity[1].wait_send()

    @pl.when(has_prev)
    def _():
        to_down[0].wait_send()
        to_down[1].wait_send()


def on_device(tiles, object_field, probe, phases, intensities, pos_row, pos_col, counts):
    side = probe.shape[1]
    cosine, sine = angle_tables(side)
    anywhere = pl.BlockSpec(memory_space=pltpu.HBM)
    block = (2, side, side)
    wide = (2 * side, 2 * side)
    dma = pltpu.SemaphoreType.DMA
    return pl.pallas_call(
        functools.partial(kernel, tiles, side),
        out_shape=jax.ShapeDtypeStruct(object_field.shape, F32),
        in_specs=[pl.BlockSpec(memory_space=pltpu.SMEM)] + [anywhere] * 8,
        out_specs=pl.BlockSpec(memory_space=pltpu.VMEM),
        scratch_shapes=[
            pltpu.SMEM((2,), jnp.int32),
            pltpu.SMEM((2,), jnp.int32),
            pltpu.VMEM((2, side, object_field.shape[3]), BF16),
            pltpu.VMEM(block, BF16),
            pltpu.VMEM((1, side), F32),
            pltpu.VMEM((side, side), F32),
            pltpu.VMEM((side, side), F32),
            pltpu.VMEM((2, side, side), BF16),
            pltpu.VMEM((8, side), jnp.int32),
            pltpu.VMEM((8, side), jnp.int32),
            pltpu.VMEM((2,) + block, BF16),
            pltpu.VMEM((2,) + block, BF16),
            pltpu.VMEM(block, BF16),
            pltpu.VMEM(block, BF16),
            pltpu.VMEM((2,) + block, BF16),
            pltpu.VMEM((2,) + block, BF16),
            pltpu.VMEM(wide, BF16),
            pltpu.VMEM(wide, BF16),
            pltpu.VMEM((2,) + wide, BF16),
            pltpu.VMEM((2,) + wide, BF16),
            pltpu.VMEM((2,) + wide, BF16),
            pltpu.VMEM((2,) + wide, BF16),
            pltpu.VMEM((2,) + block, BF16),
            pltpu.VMEM((2 * side, side), BF16),
            pltpu.VMEM((2, 2) + block, BF16),
            pltpu.VMEM((2,) + block, BF16),
            dma((8,)),
            pltpu.SemaphoreType.REGULAR,
            dma((2,)),
            dma,
            dma((2,)),
            dma((2,)),
            dma((2,)),
            dma((2,)),
            dma((2,)),
            dma((2,)),
            dma((2,)),
            dma,
            dma((2,)),
            dma((2,)),
        ],
        compiler_params=pltpu.CompilerParams(
            collective_id=0, has_side_effects=True, vmem_limit_bytes=48 * 1024 * 1024
        ),
    )(
        counts,
        *(
            pltpu.with_memory_space_constraint(value, pltpu.HBM)
            for value in (
                pos_row,
                pos_col,
                object_field,
                probe,
                phases.reshape(1, side),
                intensities,
                jnp.asarray(cosine),
                jnp.asarray(sine),
            )
        )
    )


def solution(mesh):
    placed = (
        P(None, "sec", "tile", None),
        P(),
        P(),
        P("tile", None, None),
        P("tile"),
        P("tile"),
        P("tile"),
    )
    return jax.shard_map(
        functools.partial(on_device, mesh.shape["tile"]),
        mesh=mesh,
        in_specs=placed,
        out_specs=P(None, "sec", "tile", None),
        check_vma=False,
    )
```
